32 devices in a mesh: head: 4 (over y, x), tok: 8 (over z, core).
Axes of the slice: x: 2, y: 2, z: 4, core: 2. Of those that a mesh axis runs over, the one named last changes fastest.
Arguments:
- queries: bfloat16 [2, 2048, 5120], P(None, 'tok', 'head'), may hold values from -6 to 6
- key_rows: bfloat16 [2048, 5120], P('tok', 'head'), may hold values from -6 to 6
- value_rows: bfloat16 [2048, 5120], P('tok', 'head'), may hold values from -6 to 6
- step_rates: float32 [20, 2048], P('head', 'tok'), may hold values from 0.05 to 1
- gate_fast: float32 [20, 256, 256], P('head'), may hold values from -0.375 to 0.375
- up_fast: float32 [20, 256, 256], P('head'), may hold values from -0.375 to 0.375
- down_fast: float32 [20, 256, 256], P('head'), may hold values from -0.375 to 0.375
Outputs:
- out_rows: bfloat16 [2, 2048, 5120], P(None, ('tok', 'head'))
The draws below stay inside these ranges and needn't reach their ends.
All inputs are finite; a program needn't handle non-finite values.
Results may differ from the reference program's by a relative error of at most 0.011.
Values may be sent and summed in bfloat16 or wider, within the bound.
A program may use at most 64 MiB of HBM per device.

```python
import math
import jax
import jax.numpy as jnp
from jax import lax

HD = 256
FH = 256
NS_STEPS = 3
HEADS = 20
BLOCK = 2048


def level_of(own_key, dims, cuts, smallest, largest):
    def one(axis_at, shards_of):
        draws = jax.random.uniform(jax.random.fold_in(jax.random.fold_in(own_key, 6), axis_at), (shards_of,), jnp.float32, smallest / len(cuts), largest / len(cuts))
        return jnp.repeat(jnp.exp(draws), dims[axis_at] // shards_of).reshape((-1,) + (1,) * (len(dims) - axis_at - 1))

    gain = one(*cuts[0])
    for cut in cuts[1:]:
        gain = gain * one(*cut)
    return gain


def noise(own_key, dims, deviation, most, shards=(), dtype=jnp.bfloat16):
    loudness = level_of(own_key, dims, shards, -0.22, 0.18) if shards else 1.0
    array = jax.random.normal(own_key, dims, jnp.float32) * deviation * loudness
    return jnp.minimum(jnp.maximum(array, -most), most).astype(dtype)


def setup_inputs(seed: int = 0) -> dict:
    seeds = jax.random.split(jax.random.key(seed), 8)
    queries = noise(seeds[0], (2, BLOCK, HEADS * HD), 1.0, 6.0, ((1, 8), (2, 4)))
    key_rows = noise(seeds[1], (BLOCK, HEADS * HD), 1.0, 6.0, ((0, 8), (1, 4)))
    value_rows = noise(seeds[2], (BLOCK, HEADS * HD), 1.0, 6.0, ((0, 8), (1, 4)))
    step_rates = jnp.clip(jnp.exp(math.log(1.0) - 2.9957323 * jax.random.uniform(seeds[3], (HEADS, BLOCK), jnp.float32) ** level_of(seeds[3], (HEADS, BLOCK), ((0, 4), (1, 8)), -0.2, 0.2)), 0.05, 1.0)
    gate_fast = noise(seeds[4], (HEADS, HD, FH), HD ** -0.5, 0.375, ((0, 4),), jnp.float32)
    up_fast = noise(seeds[5], (HEADS, HD, FH), HD ** -0.5, 0.375, ((0, 4),), jnp.float32)
    down_fast = noise(seeds[6], (HEADS, FH, HD), FH ** -0.5, 0.375, ((0, 4),), jnp.float32)
    return dict(queries=queries, key_rows=key_rows, value_rows=value_rows, step_rates=step_rates, gate_fast=gate_fast, up_fast=up_fast, down_fast=down_fast)


coef_first = 3.4445
coef_second = -4.775
coef_third = 2.0315

def fast_apply(inputs, gate_mat, up_mat, down_mat):
    gate_pre = jnp.dot(inputs, gate_mat, preferred_element_type=jnp.float32)
    up_pre = jnp.dot(inputs, up_mat, preferred_element_type=jnp.float32)
    hidden = (jax.nn.silu(gate_pre) * up_pre).astype(jnp.bfloat16)
    return jnp.dot(hidden, down_mat, preferred_element_type=jnp.float32).astype(jnp.bfloat16)

def orthogonal(gradient):
    iterate = gradient / (jnp.sqrt(jnp.sum(gradient * gradient)) + 1e-07)
    for sweep in range(NS_STEPS):
        gram = jnp.dot(iterate.T, iterate, precision=lax.Precision.HIGHEST)
        square = jnp.dot(gram, gram, precision=lax.Precision.HIGHEST)
        poly = coef_second * gram + coef_third * square
        iterate = coef_first * iterate + jnp.dot(iterate, poly, precision=lax.Precision.HIGHEST)
    return iterate

def head_layer(pieces):
    first_query, second_query, key_head, value_head, rates, gate_fast, up_fast, down_fast = pieces
    gate_half = gate_fast.astype(jnp.bfloat16)
    up_half = up_fast.astype(jnp.bfloat16)
    down_half = down_fast.astype(jnp.bfloat16)
    first = fast_apply(first_query, gate_half, up_half, down_half)
    gate_pre = jnp.dot(key_head, gate_half, preferred_element_type=jnp.float32)
    up_pre = jnp.dot(key_head, up_half, preferred_element_type=jnp.float32)
    sigmoid_gate = jax.nn.sigmoid(gate_pre)
    hidden = (jax.nn.silu(gate_pre) * up_pre).astype(jnp.bfloat16)
    down_in = (-(rates[:, None] * value_head.astype(jnp.float32))).astype(jnp.bfloat16)
    down_grad = jnp.dot(hidden.T, down_in, preferred_element_type=jnp.float32)
    hidden_grad = jnp.dot(down_in, down_half.T, preferred_element_type=jnp.float32)
    up_in = (hidden_grad * jax.nn.silu(gate_pre)).astype(jnp.bfloat16)
    gate_in = (hidden_grad * up_pre * sigmoid_gate * (1.0 + gate_pre * (1.0 - sigmoid_gate))).astype(jnp.bfloat16)
    gate_grad = jnp.dot(key_head.T, gate_in, preferred_element_type=jnp.float32)
    up_grad = jnp.dot(key_head.T, up_in, preferred_element_type=jnp.float32)
    gate_next = (gate_fast - orthogonal(gate_grad)).astype(jnp.bfloat16)
    up_next = (up_fast - orthogonal(up_grad)).astype(jnp.bfloat16)
    down_next = (down_fast - orthogonal(down_grad)).astype(jnp.bfloat16)
    second = fast_apply(second_query, gate_next, up_next, down_next)
    return (first, second)

def reference(queries, key_rows, value_rows, step_rates, gate_fast, up_fast, down_fast):
    query_heads = queries.reshape(2, BLOCK, HEADS, HD).transpose(2, 0, 1, 3)
    key_heads = key_rows.reshape(BLOCK, HEADS, HD).transpose(1, 0, 2)
    value_heads = value_rows.reshape(BLOCK, HEADS, HD).transpose(1, 0, 2)
    first, second = lax.map(head_layer, (query_heads[:, 0], query_heads[:, 1], key_heads, value_heads, step_rates, gate_fast, up_fast, down_fast))
    joined = jnp.stack((first, second), 0)
    return joined.transpose(0, 2, 1, 3).reshape(2, BLOCK, HEADS * HD)
```

```python
import functools

import jax
import jax.numpy as jnp
from jax import lax
from jax.experimental import pallas as pl
from jax.experimental.pallas import tpu as pltpu
from jax.sharding import PartitionSpec as P

NS_STEPS = 3
KINDS = 3
PIECES = 2
EXTRA = 2
DEPTH = 4

coef_first = 3.4445
coef_second = -4.775
coef_third = 2.0315

MESH = pl.DeviceIdType.MESH
BF = jnp.bfloat16
F32 = jnp.float32


def mm(a, b):
    return jnp.dot(a, b, preferred_element_type=F32)


def mm_tn(a, b):
    return lax.dot_general(a, b, (((0,), (0,)), ((), ())), preferred_element_type=F32)


def mm_nt(a, b):
    return lax.dot_general(a, b, (((1,), (1,)), ((), ())), preferred_element_type=F32)


def fast_apply(x, gate, up, down):
    pre = mm(x, gate)
    hidden = (pre / (1.0 + jnp.exp(-pre)) * mm(x, up)).astype(BF)
    return mm(hidden, down).astype(BF)


def kernel(
    nh, nz, q_in, k_in, v_in, rates, g_in, u_in, d_in, out,
    qb, kb, vb, wf, wh, gb, pb, cs, cr, wn, ob,
    in_sem, ps_s, ps_r, ch_s, ch_r, ag_s, ag_r, ap_s, ap_r, a_s, a_r, a_l,
):
    heads, rows, size = kb.shape
    count = KINDS * heads
    pairs = pb.shape[0]
    piece = size // PIECES
    share = rows // nh
    hd = lax.axis_index("head")
    tok = lax.axis_index("tok")
    lane = lax.rem(tok, 2)
    z = tok // 2
    partner = (hd, z * 2 + 1 - lane)

    def cut(h):
        return pl.ds(h * size if isinstance(h, int) else pl.multiple_of(h * size, size), size)

    def load(at, h):
        src, dst = (
            (k_in.at[:, cut(h)], kb.at[h]),
            (g_in.at[h], wf.at[0, h]),
            (u_in.at[h], wf.at[1, h]),
            (v_in.at[:, cut(h)], vb.at[h]),
            (d_in.at[h], wf.at[2, h]),
            (q_in.at[0, :, cut(h)], qb.at[0, h]),
            (q_in.at[1, :, cut(h)], qb.at[1, h]),
        )[at]
        return pltpu.make_async_copy(src, dst, in_sem.at[at, h])

    for h in range(heads):
        for at in range(5):
            load(at, h).start()
    for h in range(heads):
        for at in (5, 6):
            load(at, h).start()

    barrier = pltpu.get_barrier_semaphore()
    pl.semaphore_signal(barrier, inc=1, device_id=partner, device_id_type=MESH)
    for p in range(1, nh):
        pl.semaphore_signal(
            barrier, inc=1, device_id=(lax.rem(hd + p, nh), tok), device_id_type=MESH
        )

    @pl.when(z > 0)
    def _():
        pl.semaphore_signal(barrier, inc=1, device_id=(hd, tok - 2), device_id_type=MESH)

    @pl.when(z < nz - 1)
    def _():
        pl.semaphore_signal(barrier, inc=1, device_id=(hd, tok + 2), device_id_type=MESH)

    inner = (z > 0).astype(jnp.int32) + (z < nz - 1).astype(jnp.int32)
    pl.semaphore_wait(barrier, nh + inner)

    def mine(j):
        return 2 * j + lane

    def side(j):
        return lax.rem(j, 2)

    def is_start(j):
        return z == (1 - side(j)) * (nz - 1)

    def is_owner(j):
        return z == side(j) * (nz - 1)

    def towards(j):
        return (hd, tok + (2 * side(j) - 1) * 2)

    def back(j):
        return (hd, tok - (2 * side(j) - 1) * 2)

    def swap(j):
        return pltpu.make_async_remote_copy(
            gb.at[2 * j + 1 - lane], pb.at[j], ps_s.at[j], ps_r.at[j],
            device_id=partner, device_id_type=MESH,
        )

    def chain(j, g):
        part = pl.ds(g * piece, piece)
        return pltpu.make_async_remote_copy(
            cs.at[j, part], cr.at[j, part], ch_s.at[j, g], ch_r.at[j, g],
            device_id=towards(j), device_id_type=MESH,
        )

    def spread(j, g):
        part = pl.ds(g * piece, piece)
        return pltpu.make_async_remote_copy(
            wn.at[mine(j), part], wn.at[mine(j), part], ag_s.at[j, g], ag_r.at[j, g],
            device_id=back(j), device_id_type=MESH,
        )

    def across(j, g, m):
        part = pl.ds(g * piece, piece)
        return pltpu.make_async_remote_copy(
            wn.at[m, part], wn.at[m, part], ap_s.at[j, g], ap_r.at[j, g],
            device_id=partner, device_id_type=MESH,
        )

    def launch(make, j, g):
        before = j + 2 * ((g - DEPTH) // PIECES)

        @pl.when(before >= 0)
        def _():
            make(before, (g - DEPTH) % PIECES).wait_send()

        make(j, g).start()

    def land(make, j, g):
        @pl.when(mine(j + 2 * ((g + DEPTH) // PIECES)) >= count)
        def _():
            make(j, g).wait_send()

    def wide(h):
        return pl.ds(pl.multiple_of((hd * heads + h) * size, size), size)

    def deal(b, h, p):
        peer = lax.rem(hd + p, nh)
        return pltpu.make_async_remote_copy(
            ob.at[b, h, pl.ds(pl.multiple_of(peer * share, share), share)],
            out.at[b, :, wide(h)],
            a_s.at[b, h, p - 1], a_r.at[b, h, p - 1],
            device_id=(peer, tok), device_id_type=MESH,
        )

    def arrive(b, h, p):
        source = lax.rem(hd + nh - p, nh)
        return pltpu.make_async_remote_copy(
            ob.at[b, h, pl.ds(pl.multiple_of(hd * share, share), share)],
            out.at[b, :, pl.ds(pl.multiple_of((source * heads + h) * size, size), size)],
            a_s.at[b, h, p - 1], a_r.at[b, h, p - 1],
            device_id=(source, tok), device_id_type=MESH,
        )

    def keep(b, h):
        return pltpu.make_async_copy(
            ob.at[b, h, pl.ds(pl.multiple_of(hd * share, share), share)],
            out.at[b, :, wide(h)], a_l.at[b, h],
        )

    def deal_all(b, h):
        for p in range(nh - 1, 0, -1):
            deal(b, h, p).start()
        keep(b, h).start()

    def wait_load(h, picks):
        for at in picks:
            load(at, h).wait()

    def gradients(h):
        wait_load(h, range(5))
        keys = kb[h]
        gate = wf[0, h].astype(BF)
        up = wf[1, h].astype(BF)
        down = wf[2, h].astype(BF)
        wh[0, h] = gate
        wh[1, h] = up
        wh[2, h] = down
        zg = mm(keys, gate)
        zu = mm(keys, up)
        sig = 1.0 / (1.0 + jnp.exp(-zg))
        silu = zg * sig
        hidden = (silu * zu).astype(BF)
        line = jnp.broadcast_to(rates[pl.ds(h, 1), :], (128, rows))
        column = jnp.transpose(line)
        column = jnp.concatenate([column] * (size // 128), axis=1)
        dout = (-(column * vb[h].astype(F32))).astype(BF)
        dh = mm_nt(dout, down)
        dzu = (dh * silu).astype(BF)
        dzg = (dh * zu * sig * (1.0 + zg * (1.0 - sig))).astype(BF)
        base = KINDS * h
        gb[base] = mm_tn(keys, dzg).astype(BF)
        gb[base + 1] = mm_tn(keys, dzu).astype(BF)
        gb[base + 2] = mm_tn(hidden, dout).astype(BF)
        for kind in range(KINDS):
            m = base + kind

            @pl.when(lax.rem(m, 2) != lane)
            def _():
                swap(m // 2).start()

    def first(h):
        wait_load(h, (5,))
        ob[0, h] = fast_apply(qb[0, h], wh[0, h], wh[1, h], wh[2, h])
        deal_all(0, h)

    def own(h, step):
        for kind in range(KINDS):
            m = KINDS * h + kind

            @pl.when(lax.rem(m, 2) == lane)
            def _():
                step(m // 2)

    def start_step(j):
        swap(j).wait_recv()

        @pl.when(is_start(j))
        def _():
            cs[j] = (gb[mine(j)].astype(F32) + pb[j].astype(F32)).astype(BF)
            for g in range(PIECES):
                launch(chain, j, g)

    def pass_step(j):
        @pl.when(jnp.logical_not(is_start(j)) & jnp.logical_not(is_owner(j)))
        def _():
            for g in range(PIECES):
                part = pl.ds(g * piece, piece)
                chain(j, g).wait_recv()
                cs[j, part] = (
                    gb[mine(j), part].astype(F32)
                    + pb[j, part].astype(F32)
                    + cr[j, part].astype(F32)
                ).astype(BF)
                launch(chain, j, g)

    lag = EXTRA + max(
        min((2 * j + 1) // KINDS, heads - 1) + 1 - (j // 2 + 1) for j in range(pairs)
    )
    turns = (pairs - 1) // 2 + nz - 1
    total = max(2 * heads, turns + lag)

    def reach(j):
        return jnp.where(side(j) == 0, nz - 1 - z, z)

    @pl.loop(0, total)
    def _(t):
        @pl.when(t < heads)
        def _():
            gradients(t)

        @pl.when((t >= heads) & (t < 2 * heads))
        def _():
            first(t - heads)

        @pl.when((t >= 1) & (t <= heads))
        def _():
            own(t - 1, start_step)

        for s in range(2):
            i = t - lag - reach(s)
            j = 2 * i + s

            @pl.when((i >= 0) & (j < pairs) & (mine(j) < count))
            def _():
                pass_step(j)

    @pl.loop(0, pairs)
    def _(j):
        m = mine(j)

        @pl.when((m < count) & is_owner(j))
        def _():
            for g in range(PIECES):
                chain(j, g).wait_recv()
            grad = gb[m].astype(F32) + pb[j].astype(F32) + cr[j].astype(F32)
            scale = jnp.sqrt(jnp.sum(grad * grad)) + 1e-07
            x = grad / scale
            for _ in range(NS_STEPS):
                xb = x.astype(BF)
                gram = mm_tn(xb, xb)
                half = gram.astype(BF)
                poly = coef_second * gram + coef_third * mm(half, half)
                x = coef_first * x + mm(xb, poly.astype(BF))
            wn[m] = (wf[lax.rem(m, KINDS), m // KINDS] - x).astype(BF)
            for g in range(PIECES):
                launch(spread, j, g)
                across(j, g, m).start()

    def second(h):
        for kind in range(KINDS):
            m = KINDS * h + kind

            @pl.when(lax.rem(m, 2) != lane)
            def _():
                for g in range(PIECES):
                    across(m // 2, g, m).wait_recv()

        wait_load(h, (6,))
        base = KINDS * h
        ob[1, h] = fast_apply(qb[1, h], wn[base], wn[base + 1], wn[base + 2])
        deal_all(1, h)

    def relay(j):
        m = mine(j)
        for g in range(PIECES):
            spread(j, g).wait_recv()

            @pl.when(jnp.logical_not(is_start(j)))
            def _():
                launch(spread, j, g)

            across(j, g, m).start()

    def away(j):
        return jnp.where(side(j) == 0, z, nz - 1 - z)

    @pl.loop(0, (pairs - 1) // 2 + nz)
    def _(t):
        for s in range(2):
            i = t - away(s)
            j = 2 * i + s

            @pl.when((i >= 0) & (j < pairs) & (mine(j) < count) & jnp.logical_not(is_owner(j)))
            def _():
                relay(j)

        @pl.loop(0, heads)
        def _(h):
            top = (KINDS * h + KINDS - 1) // 2
            below = top - 1
            due = jnp.maximum(top // 2 + away(top), below // 2 + away(below))

            @pl.when(due == t)
            def _():
                second(h)

    @pl.loop(0, pairs)
    def _(j):
        m = mine(j)

        @pl.when(2 * j + 1 - lane < count)
        def _():
            swap(j).wait_send()

        @pl.when(m < count)
        def _():
            for g in range(PIECES):
                across(j, g, m).wait_send()

                @pl.when(jnp.logical_not(is_owner(j)))
                def _():
                    land(chain, j, g)

                @pl.when(jnp.logical_not(is_start(j)))
                def _():
                    land(spread, j, g)

    for b in range(2):
        @pl.loop(0, heads)
        def _(h):
            for p in range(1, nh):
                arrive(b, h, p).wait_recv()
                deal(b, h, p).wait_send()
            keep(b, h).wait()


def solution(mesh):
    nh = mesh.shape["head"]
    nz = mesh.shape["tok"] // 2

    def local(queries, key_rows, value_rows, step_rates, gate_fast, up_fast, down_fast):
        heads, size, _ = gate_fast.shape
        rows = key_rows.shape[0]
        pairs = (KINDS * heads + 1) // 2
        anywhere = pl.BlockSpec(memory_space=pl.ANY)
        dma = pltpu.SemaphoreType.DMA
        return pl.pallas_call(
            functools.partial(kernel, nh, nz),
            out_shape=pltpu.VMEM((2, rows // nh, nh * heads * size), BF),
            in_specs=[
                anywhere, anywhere, anywhere,
                pl.BlockSpec(memory_space=pltpu.VMEM),
                anywhere, anywhere, anywhere,
            ],
            out_specs=pl.BlockSpec(memory_space=pltpu.VMEM),
            scratch_shapes=[
                pltpu.VMEM((2, heads, rows, size), BF),
                pltpu.VMEM((heads, rows, size), BF),
                pltpu.VMEM((heads, rows, size), BF),
                pltpu.VMEM((KINDS, heads, size, size), F32),
                pltpu.VMEM((KINDS, heads, size, size), BF),
                pltpu.VMEM((2 * pairs, size, size), BF),
                pltpu.VMEM((pairs, size, size), BF),
                pltpu.VMEM((pairs, size, size), BF),
                pltpu.VMEM((pairs, size, size), BF),
                pltpu.VMEM((2 * pairs, size, size), BF),
                pltpu.VMEM((2, heads, rows, size), BF),
                dma((7, heads)),
                dma((pairs,)), dma((pairs,)),
                dma((pairs, PIECES)), dma((pairs, PIECES)),
                dma((pairs, PIECES)), dma((pairs, PIECES)),
                dma((pairs, PIECES)), dma((pairs, PIECES)),
                dma((2, heads, nh - 1)), dma((2, heads, nh - 1)),
                dma((2, heads)),
            ],
            compiler_params=pltpu.CompilerParams(
                collective_id=0, has_side_effects=True, vmem_limit_bytes=67043328-1310720-16384
            ),
        )(queries, key_rows, value_rows, step_rates, gate_fast, up_fast, down_fast)

    placed = (
        P(None, "tok", "head"),
        P("tok", "head"),
        P("tok", "head"),
        P("head", "tok"),
        P("head", None, None),
        P("head", None, None),
        P("head", None, None),
    )
    return jax.shard_map(
        local, mesh=mesh, in_specs=placed, out_specs=P(None, ("tok", "head"), None), check_vma=False
    )
```

```python
import functools

import jax
import jax.numpy as jnp
from jax import lax
from jax.experimental import pallas as pl
from jax.experimental.pallas import tpu as pltpu
from jax.sharding import PartitionSpec as P

NS_STEPS = 3
KINDS = 3
PIECES = 4
LAG = 5
LAG_ALONE = 9
VMEM_BYTES = 67043328

coef_first = 3.4445
coef_second = -4.775
coef_third = 2.0315

MESH = pl.DeviceIdType.MESH
BF = jnp.bfloat16
F32 = jnp.float32


def mm(a, b):
    return jnp.dot(a, b, preferred_element_type=F32)


def mm_tn(a, b):
    return lax.dot_general(a, b, (((0,), (0,)), ((), ())), preferred_element_type=F32)


def mm_nt(a, b):
    return lax.dot_general(a, b, (((1,), (1,)), ((), ())), preferred_element_type=F32)


def fast_apply(x, gate, up, down):
    pre = mm(x, gate)
    hidden = (pre / (1.0 + jnp.exp(-pre)) * mm(x, up)).astype(BF)
    return mm(hidden, down).astype(BF)


def kernel(
    nh, nz, q_in, k_in, v_in, r_in, g_in, u_in, d_in, out,
    qb, qn, kb, vb, rb, wf, wh, own, sent, got, pi, si, po, so, mg, xs, gm, pm, wn, ob, ox,
    ld, qs, sw_s, sw_r, p_s, p_r, s_s, s_r, a_s, a_r, b_s, b_r, b_p, b_l,
):
    heads, share, size = ob.shape[0], ob.shape[1] // nh, ob.shape[2]
    rows = nh * share
    slots = sent.shape[0]
    piece = size // PIECES
    per = KINDS * PIECES
    hd = lax.axis_index("head")
    tok = lax.axis_index("tok")
    lane = lax.rem(tok, 2)
    z = tok // 2
    partner = (hd, z * 2 + 1 - lane)
    total = per * ((heads + 1 - lane) // 2)
    first_end = z == 0
    last_end = z == nz - 1
    middle = jnp.logical_not(first_end) & jnp.logical_not(last_end)

    def cut(h):
        return pl.ds(h * size if isinstance(h, int) else pl.multiple_of(h * size, size), size)

    def mine(i):
        return 2 * i + lane

    def theirs(i):
        return 2 * i + 1 - lane

    barrier = pltpu.get_barrier_semaphore()

    @pl.when(z > 0)
    def _():
        pl.semaphore_signal(barrier, inc=1, device_id=(hd, tok - 2), device_id_type=MESH)

    @pl.when(z < nz - 1)
    def _():
        pl.semaphore_signal(barrier, inc=1, device_id=(hd, tok + 2), device_id_type=MESH)

    pl.semaphore_signal(barrier, inc=1, device_id=partner, device_id_type=MESH)
    for p in range(1, nh):
        for c in range(2):
            pl.semaphore_signal(
                barrier, inc=1, device_id=(lax.rem(hd + p, nh), 2 * z + c), device_id_type=MESH
            )
    inner = (z > 0).astype(jnp.int32) + (z < nz - 1).astype(jnp.int32)

    def load_head(stage, columns, some):
        pltpu.make_async_copy(k_in.at[:, columns], kb.at[:, columns], ld.at[stage, 0]).start()
        for k, src in enumerate((g_in, u_in)):
            pltpu.make_async_copy(src.at[some], wf.at[k, some], ld.at[stage, 1]).start()
        pltpu.make_async_copy(v_in.at[:, columns], vb.at[:, columns], ld.at[stage, 0]).start()
        pltpu.make_async_copy(d_in.at[some], wf.at[2, some], ld.at[stage, 1]).start()

    def wait_head(stage, count):
        both = q_in.at[:, :, pl.ds(0, count * size)]
        pltpu.make_async_copy(both, both, ld.at[stage, 0]).wait()
        three = wf.at[:, pl.ds(0, count)]
        pltpu.make_async_copy(three, three, ld.at[stage, 1]).wait()

    load_rates = pltpu.make_async_copy(r_in, rb, ld.at[3, 0])
    load_first = pltpu.make_async_copy(q_in.at[0], qb, ld.at[3, 1])
    load_next = pltpu.make_async_copy(q_in.at[1], qn.at[lane], ld.at[4, 0])
    push_next = pltpu.make_async_remote_copy(
        q_in.at[1], qn.at[lane], qs.at[0], qs.at[1], device_id=partner, device_id_type=MESH
    )

    def place(t):
        return t // PIECES, pl.ds(pl.multiple_of(lax.rem(t, PIECES) * piece, piece), piece)

    def right(src, t):
        m, part = place(t)
        return pltpu.make_async_remote_copy(
            src.at[m, part], pi.at[m, part], p_s.at[t // per], p_r.at[t],
            device_id=(hd, tok + 2), device_id_type=MESH,
        )

    def left(src, t):
        m, part = place(t)
        return pltpu.make_async_remote_copy(
            src.at[m, part], si.at[m, part], s_s.at[t // per], s_r.at[t],
            device_id=(hd, tok - 2), device_id_type=MESH,
        )

    def swap(i, k):
        return pltpu.make_async_remote_copy(
            sent.at[i, k], got.at[i, k], sw_s.at[i], sw_r.at[i, k],
            device_id=partner, device_id_type=MESH,
        )

    def wide(h):
        return pl.ds(pl.multiple_of((hd * heads + h) * size, size), size)

    def band(peer):
        return pl.ds(pl.multiple_of(peer * share, share), share)

    order = (3, 1, 2, 0) if nh == 4 else tuple(range(nh - 1, -1, -1))

    def other(p):
        if nh != 4 or p == 0:
            return lax.rem(hd + p, nh)
        return (hd + 1 - 2 * lax.rem(hd, 2), lax.rem(hd + 2, 4), 3 - hd)[p - 1]

    def deal(h, p):
        peer = other(p)
        return pltpu.make_async_remote_copy(
            ob.at[h, band(peer)], out.at[0, :, wide(h)], a_s.at[0], a_r.at[p - 1],
            device_id=(peer, tok), device_id_type=MESH,
        )

    def keep(h):
        return pltpu.make_async_copy(ob.at[h, band(hd)], out.at[0, :, wide(h)], a_s.at[1])

    def deal_next(i, c, p):
        peer = other(p)
        return pltpu.make_async_remote_copy(
            ox.at[i, c * nh + peer], out.at[1, :, wide(mine(i))],
            b_s.at[i], b_p.at[i] if p == 0 else b_r.at[p - 1],
            device_id=(peer, 2 * z + c), device_id_type=MESH,
        )

    def keep_next(i):
        return pltpu.make_async_copy(
            ox.at[i, lane * nh + hd], out.at[1, :, wide(mine(i))], b_l.at[i]
        )

    def gradients(h):
        keys = kb[:, cut(h)]
        gate = wf[0, h].astype(BF)
        up = wf[1, h].astype(BF)
        down = wf[2, h].astype(BF)
        wh[0, h] = gate
        wh[1, h] = up
        wh[2, h] = down
        zg = mm(keys, gate)
        zu = mm(keys, up)
        sig = 1.0 / (1.0 + jnp.exp(-zg))
        silu = zg * sig
        hidden = (silu * zu).astype(BF)
        line = jnp.broadcast_to(rb[pl.ds(h, 1), :], (128, rows))
        column = jnp.transpose(line)
        column = jnp.concatenate([column] * (size // 128), axis=1)
        dout = (-(column * vb[:, cut(h)].astype(F32))).astype(BF)
        dh = mm_nt(dout, down)
        dzu = (dh * silu).astype(BF)
        dzg = (dh * zu * sig * (1.0 + zg * (1.0 - sig))).astype(BF)
        return mm_tn(keys, dzg), mm_tn(keys, dzu), mm_tn(hidden, dout)

    def gradients_theirs(i):
        parts = gradients(theirs(i))
        for k in range(KINDS):
            sent[i, k] = parts[k].astype(BF)

    def gradients_mine(i):
        parts = gradients(mine(i))
        for k in range(KINDS):
            mg[k] = parts[k]

    def add_theirs(i):
        for k in range(KINDS):
            swap(i, k).wait_recv()
            own[KINDS * i + k] = (mg[k] + got[i, k].astype(F32)).astype(BF)

            @pl.when(first_end)
            def _():
                for g in range(PIECES):
                    right(own, per * i + k * PIECES + g).start()

            @pl.when(last_end)
            def _():
                for g in range(PIECES):
                    left(own, per * i + k * PIECES + g).start()

    turn_at = per * (slots - 1)
    alone = (mine(slots - 1) < heads) & (theirs(slots - 1) >= heads)

    def turn(t, far):
        fast = (LAG_ALONE - LAG) * far
        held = jnp.where(t < turn_at + fast, -1, t - LAG_ALONE * far)
        return jnp.where(alone & (t >= turn_at), held, t - LAG * far)

    def pass_on(t):
        p = turn(t, z - 1)
        s = turn(t, nz - 2 - z)

        @pl.when(middle & (p >= 0) & (p < total))
        def _():
            m, part = place(p)
            right(po, p).wait_recv()
            po[m, part] = (pi[m, part].astype(F32) + own[m, part].astype(F32)).astype(BF)
            right(po, p).start()

        @pl.when(middle & (s >= 0) & (s < total))
        def _():
            m, part = place(s)
            left(so, s).wait_recv()
            so[m, part] = (si[m, part].astype(F32) + own[m, part].astype(F32)).astype(BF)
            left(so, s).start()

    def first(h):
        ob[h] = fast_apply(qb[:, cut(h)], wh[0, h], wh[1, h], wh[2, h])
        for p in order[:-1]:
            deal(h, p).start()
        keep(h).start()

    def gather_some(i, kinds):
        for k in kinds:
            m = KINDS * i + k

            @pl.when(first_end)
            def _():
                for g in range(PIECES):
                    left(own, per * i + k * PIECES + g).wait_recv()
                xs[k] = own[m].astype(F32) + si[m].astype(F32)

            @pl.when(last_end)
            def _():
                for g in range(PIECES):
                    right(own, per * i + k * PIECES + g).wait_recv()
                xs[k] = own[m].astype(F32) + pi[m].astype(F32)

            @pl.when(middle)
            def _():
                xs[k] = own[m].astype(F32) + pi[m].astype(F32) + si[m].astype(F32)

        grads = [xs[k] for k in kinds]
        scales = [1.0 / (jnp.sqrt(jnp.sum(v * v)) + 1e-07) for v in grads]
        for k, v, scale in zip(kinds, grads, scales):
            xs[k] = v * scale

    def gather(i):
        gather_some(i, range(KINDS - 1))
        gather_some(i, [KINDS - 1])

    def gram_all():
        for k in range(KINDS):
            x = xs[k].astype(BF)
            gm[k] = mm_nt(x, x)

    def poly_all():
        for k in range(KINDS):
            half = gm[k].astype(BF)
            pm[k] = (coef_second * gm[k] + coef_third * mm(half, half)).astype(BF)

    def apply_all():
        for k in range(KINDS):
            xs[k] = coef_first * xs[k] + mm(pm[k], xs[k].astype(BF))

    def sweep():
        x = [xs[k] for k in range(KINDS)]
        xb = [v.astype(BF) for v in x]
        gram = [mm_nt(v, v) for v in xb]
        half = [v.astype(BF) for v in gram]
        square = [mm(v, v) for v in half]
        poly = [(coef_second * a + coef_third * b).astype(BF) for a, b in zip(gram, square)]
        for k in range(KINDS):
            xs[k] = coef_first * x[k] + mm(poly[k], xb[k])

    def update(i):
        for k in range(KINDS):
            wn[k] = (wf[k, mine(i)] - xs[k]).astype(BF)

    def second(i):
        x = qn[:, :, cut(mine(i))].reshape(2 * rows, size)
        ox[i] = fast_apply(x, wn[0], wn[1], wn[2]).reshape(2 * nh, share, size)
        for p in order:
            for c in range(2):
                if p > 0:
                    deal_next(i, c, p).start()
                else:

                    @pl.when(lane != c)
                    def _():
                        deal_next(i, c, p).start()

        keep_next(i).start()

    def ready_theirs(i):
        @pl.when(theirs(i) < heads)
        def _():
            gradients_theirs(i)
            for k in range(KINDS):
                swap(i, k).start()

    def add_mine(i):
        @pl.when(mine(i) < heads)
        def _():
            add_theirs(i)

    def ready_mine(i):
        @pl.when((i < slots) & (mine(i) < heads))
        def _():
            gradients_mine(i)
            add_theirs(i)

    def first_of(h):
        @pl.when(h < heads)
        def _():
            first(h)

    load_rates.start()
    load_head(0, cut(theirs(0)), pl.ds(theirs(0), 1))
    load_head(1, cut(mine(0)), pl.ds(mine(0), 1))
    load_rates.wait()
    wait_head(0, 1)
    if heads > 2:
        rest = heads - 2
        load_head(2, pl.ds(2 * size, rest * size), pl.ds(2, rest))
    load_first.start()
    load_next.start()
    gradients_theirs(0)
    wait_head(1, 1)
    gradients_mine(0)
    pl.semaphore_wait(barrier, 1 + 2 * (nh - 1) + inner)
    for k in range(KINDS):
        swap(0, k).start()
    add_theirs(0)
    if heads > 2:
        wait_head(2, rest)

        @pl.loop(1, slots)
        def _(i):
            ready_theirs(i)

    push_next.start()
    if slots > 1:

        @pl.when(mine(1) < heads)
        def _():
            gradients_mine(1)

    hops = max(nz - 3, 0)
    late = LAG * hops if turn_at - LAG * hops >= per * (slots - 2) else LAG_ALONE * hops
    behind, offset = late // per, late % per
    defer = middle & (mine(slots - 1) < heads)

    def finish(i):
        update(i)
        second(i)

    load_first.wait()

    @pl.loop(0, slots + behind)
    def _(r):
        base = per * r
        i = r - 1 - behind

        def done(work):
            def run():
                @pl.when((i >= 0) & jnp.logical_not(defer & (i == slots - 2)))
                def _():
                    work()

            return run

        def begin():
            @pl.when(i == 0)
            def _():
                load_next.wait()
                push_next.wait_recv()

            gather(i)

        start = offset
        work = {1: [lambda: ready_mine(r + 2)]}
        firsts = (heads + 1) // 2
        for n in range(firsts):
            work[2 * n + 3] = [lambda n=n: first_of(firsts * r + n)]
        tail = []
        for n, item in enumerate([begin, None, sweep, sweep, None, sweep, lambda: finish(i)]):
            if item is None:
                continue
            if start + n < per:
                work.setdefault(start + n, []).append(done(item))
            else:
                tail.append(done(item))
        for t in range(per):
            pass_on(base + t)
            if t == 0 and slots > 1:

                @pl.when(r == 0)
                def _():
                    add_mine(1)

            for item in work.get(t, []):
                item()
        for item in tail:
            item()

    def last_wait(i):
        if slots <= 2:

            @pl.when(i == 0)
            def _():
                load_next.wait()
                push_next.wait_recv()

    begun = per * (slots + behind)
    ended = per * slots + LAG_ALONE * hops
    held = max(slots - 2, 0)
    small = [lambda k=k: gather_some(held, [k]) for k in range(KINDS)]
    small += [gram_all, poly_all, apply_all] * NS_STEPS
    if nz == 4 and slots > 1:
        for t in range(begun, ended):
            pass_on(t)

            @pl.when(defer)
            def _():
                if t == begun:
                    last_wait(held)
                n = t - begun
                for run in small[n * len(small) // (ended - begun) : (n + 1) * len(small) // (ended - begun)]:
                    run()
    else:

        @pl.loop(begun, ended)
        def _(t):
            pass_on(t)

        @pl.when(defer)
        def _():
            last_wait(held)
            for run in small:
                run()

    @pl.when(defer)
    def _():
        if slots > 1:
            finish(held)

    @pl.when(mine(slots - 1) < heads)
    def _():
        if slots == 1:
            last_wait(0)
        gather(slots - 1)
        for s in range(NS_STEPS):
            sweep()
        finish(slots - 1)

    push_next.wait_send()

    @pl.loop(0, slots)
    def _(i):
        @pl.when(theirs(i) < heads)
        def _():
            pltpu.make_async_copy(sent.at[i], sent.at[i], sw_s.at[i]).wait()
            part = ox.at[i, 0]
            pltpu.make_async_copy(part, part, b_p.at[i]).wait()

        @pl.when(mine(i) < heads)
        def _():
            part = ox.at[i, pl.ds(0, 2 * nh - 1)]
            pltpu.make_async_copy(part, part, b_s.at[i]).wait()
            keep_next(i).wait()
            slot = own.at[pl.ds(KINDS * i, KINDS)]

            @pl.when(z < nz - 1)
            def _():
                pltpu.make_async_copy(slot, slot, p_s.at[i]).wait()

            @pl.when(z > 0)
            def _():
                pltpu.make_async_copy(slot, slot, s_s.at[i]).wait()

    part = ob.at[:, pl.ds(0, (nh - 1) * share)]
    pltpu.make_async_copy(part, part, a_s.at[0]).wait()
    part = ob.at[:, pl.ds(0, share)]
    pltpu.make_async_copy(part, part, a_s.at[1]).wait()
    for p in range(1, nh):
        part = out.at[0, :, pl.ds(0, heads * size)]
        pltpu.make_async_copy(part, part, a_r.at[p - 1]).wait()
        part = out.at[1, :, pl.ds(0, heads * size)]
        pltpu.make_async_copy(part, part, b_r.at[p - 1]).wait()


def solution(mesh):
    nh = mesh.shape["head"]
    nz = mesh.shape["tok"] // 2

    def local(queries, key_rows, value_rows, step_rates, gate_fast, up_fast, down_fast):
        heads, size, _ = gate_fast.shape
        rows = key_rows.shape[0]
        slots = (heads + 1) // 2
        matrices = KINDS * slots
        pieces = matrices * PIECES
        out_shape = (2, rows // nh, nh * heads * size)
        out_bytes = 2 * out_shape[0] * out_shape[1] * out_shape[2]
        anywhere = pl.BlockSpec(memory_space=pl.ANY)
        dma = pltpu.SemaphoreType.DMA
        stack = pltpu.VMEM((matrices, size, size), BF)
        return pl.pallas_call(
            functools.partial(kernel, nh, nz),
            out_shape=pltpu.VMEM(out_shape, BF),
            in_specs=[anywhere] * 7,
            out_specs=pl.BlockSpec(memory_space=pltpu.VMEM),
            scratch_shapes=[
                pltpu.VMEM((rows, heads * size), BF),
                pltpu.VMEM((2, rows, heads * size), BF),
                pltpu.VMEM((rows, heads * size), BF),
                pltpu.VMEM((rows, heads * size), BF),
                pltpu.VMEM((heads, rows), F32),
                pltpu.VMEM((KINDS, heads, size, size), F32),
                pltpu.VMEM((KINDS, heads, size, size), BF),
                stack,
                pltpu.VMEM((slots, KINDS, size, size), BF),
                pltpu.VMEM((slots, KINDS, size, size), BF),
                stack, stack, stack, stack,
                pltpu.VMEM((KINDS, size, size), F32),
                pltpu.VMEM((KINDS, size, size), F32),
                pltpu.VMEM((KINDS, size, size), F32),
                pltpu.VMEM((KINDS, size, size), BF),
                pltpu.VMEM((KINDS, size, size), BF),
                pltpu.VMEM((heads, rows, size), BF),
                pltpu.VMEM((slots, 2 * nh, rows // nh, size), BF),
                dma((5, 2)),
                dma((2,)),
                dma((slots,)), dma((slots, KINDS)),
                dma((slots,)), dma((pieces,)),
                dma((slots,)), dma((pieces,)),
                dma((2,)), dma((nh - 1,)),
                dma((slots,)), dma((nh - 1,)), dma((slots,)), dma((slots,)),
            ],
            compiler_params=pltpu.CompilerParams(
                collective_id=0,
                has_side_effects=True,
                vmem_limit_bytes=VMEM_BYTES - out_bytes - 16384,
            ),
        )(queries, key_rows, value_rows, step_rates, gate_fast, up_fast, down_fast)

    placed = (
        P(None, "tok", "head"),
        P("tok", "head"),
        P("tok", "head"),
        P("head", "tok"),
        P("head", None, None),
        P("head", None, None),
        P("head", None, None),
    )
    return jax.shard_map(
        local, mesh=mesh, in_specs=placed, out_specs=P(None, ("tok", "head"), None), check_vma=False
    )
```

```python
import functools

import jax
import jax.numpy as jnp
from jax import lax
from jax.experimental import pallas as pl
from jax.experimental.pallas import tpu as pltpu
from jax.sharding import PartitionSpec as P

NS_STEPS = 3
KINDS = 3
PIECES = 4
PAIR = 2
LAG = 5
LAG_ALONE = 9
VMEM_BYTES = 67043328

coef_first = 3.4445
coef_second = -4.775
coef_third = 2.0315

MESH = pl.DeviceIdType.MESH
BF = jnp.bfloat16
F32 = jnp.float32


def mm(a, b):
    return jnp.dot(a, b, preferred_element_type=F32)


def mm_tn(a, b):
    return lax.dot_general(a, b, (((0,), (0,)), ((), ())), preferred_element_type=F32)


def mm_nt(a, b):
    return lax.dot_general(a, b, (((1,), (1,)), ((), ())), preferred_element_type=F32)


def fast_apply(x, gate, up, down):
    pre = mm(x, gate)
    hidden = (pre / (1.0 + jnp.exp(-pre)) * mm(x, up)).astype(BF)
    return mm(hidden, down).astype(BF)


def kernel(
    nh, nz, q_in, k_in, v_in, r_in, g_in, u_in, d_in, out,
    qb, qn, kb, vb, rb, wf, wh, own, sent, got, pi, si, po, so, mg, xs, wn, ob, ox,
    ld, qs, sw_s, sw_p, sw_r, p_s, p_r, s_s, s_r, a_s, a_r, b_s, b_r, b_p, b_l,
):
    heads, share, size = ob.shape[0], ob.shape[1] // nh, ob.shape[2]
    rows = nh * share
    slots = sent.shape[0]
    piece = size // PIECES
    per = KINDS * PIECES
    hd = lax.axis_index("head")
    tok = lax.axis_index("tok")
    lane = lax.rem(tok, 2)
    z = tok // 2
    partner = (hd, z * 2 + 1 - lane)
    total = per * ((heads + 1 - lane) // 2)
    first_end = z == 0
    last_end = z == nz - 1
    middle = jnp.logical_not(first_end) & jnp.logical_not(last_end)

    def cut(h):
        return pl.ds(h * size if isinstance(h, int) else pl.multiple_of(h * size, size), size)

    def mine(i):
        return 2 * i + lane

    def theirs(i):
        return 2 * i + 1 - lane

    barrier = pltpu.get_barrier_semaphore()

    @pl.when(z > 0)
    def _():
        pl.semaphore_signal(barrier, inc=1, device_id=(hd, tok - 2), device_id_type=MESH)

    @pl.when(z < nz - 1)
    def _():
        pl.semaphore_signal(barrier, inc=1, device_id=(hd, tok + 2), device_id_type=MESH)

    inner = (z > 0).astype(jnp.int32) + (z < nz - 1).astype(jnp.int32)

    def greet_plane():
        pl.semaphore_signal(barrier, inc=1, device_id=partner, device_id_type=MESH)
        for p in range(1, nh):
            for c in range(2):
                pl.semaphore_signal(
                    barrier, inc=1, device_id=(lax.rem(hd + p, nh), 2 * z + c), device_id_type=MESH
                )

    def load_head(stage, columns, some):
        pltpu.make_async_copy(k_in.at[:, columns], kb.at[:, columns], ld.at[stage, 0]).start()
        for k, src in ((1, g_in), (2, u_in)):
            pltpu.make_async_copy(src.at[some], wf.at[k, some], ld.at[stage, 1]).start()
        pltpu.make_async_copy(v_in.at[:, columns], vb.at[:, columns], ld.at[stage, 0]).start()
        pltpu.make_async_copy(d_in.at[some], wf.at[0, some], ld.at[stage, 1]).start()

    def wait_head(stage, count):
        both = q_in.at[:, :, pl.ds(0, count * size)]
        pltpu.make_async_copy(both, both, ld.at[stage, 0]).wait()
        three = wf.at[:, pl.ds(0, count)]
        pltpu.make_async_copy(three, three, ld.at[stage, 1]).wait()

    def opening():
        h = theirs(0)
        some = pl.ds(h, 1)
        keys = pltpu.make_async_copy(k_in.at[:, cut(h)], kb.at[:, cut(h)], ld.at[0, 0])
        values = pltpu.make_async_copy(v_in.at[:, cut(h)], vb.at[:, cut(h)], ld.at[0, 1])
        gates = pltpu.make_async_copy(g_in.at[some], wf.at[1, some], ld.at[3, 1])
        ups = pltpu.make_async_copy(u_in.at[some], wf.at[2, some], ld.at[3, 1])
        downs = pltpu.make_async_copy(d_in.at[some], wf.at[0, some], ld.at[4, 1])
        return keys, gates, ups, values, downs, load_rates

    load_rates = pltpu.make_async_copy(r_in, rb, ld.at[3, 0])
    load_first = pltpu.make_async_copy(q_in.at[0], qb, ld.at[4, 0])
    load_next = pltpu.make_async_copy(q_in.at[1], qn.at[lane], ld.at[4, 0])
    load_both = pltpu.make_async_copy(q_in, q_in, ld.at[4, 0])
    push_next = pltpu.make_async_remote_copy(
        q_in.at[1], qn.at[lane], qs.at[0], qs.at[1], device_id=partner, device_id_type=MESH
    )

    def place(t):
        return t // PIECES, pl.ds(pl.multiple_of(lax.rem(t, PIECES) * piece, piece), piece)

    def place_right(t):
        span = PAIR * piece
        each = PIECES // PAIR
        return t // each, pl.ds(pl.multiple_of(lax.rem(t, each) * span, span), span)

    def right(src, t):
        m, part = place_right(t)
        return pltpu.make_async_remote_copy(
            src.at[m, part], pi.at[m, part], p_s.at[t // (per // PAIR)], p_r.at[t],
            device_id=(hd, tok + 2), device_id_type=MESH,
        )

    def left(src, t):
        m, part = place(t)
        return pltpu.make_async_remote_copy(
            src.at[m, part], si.at[m, part], s_s.at[t // per], s_r.at[t],
            device_id=(hd, tok - 2), device_id_type=MESH,
        )

    def swap(i, k):
        return pltpu.make_async_remote_copy(
            sent.at[i, k], got.at[i, k], sw_s.at[i], sw_r.at[i],
            device_id=partner, device_id_type=MESH,
        )

    def swap_piece(g):
        part = pl.ds(g * piece, piece)
        return pltpu.make_async_remote_copy(
            sent.at[0, 0, part], got.at[0, 0, part], sw_s.at[0], sw_p.at[g],
            device_id=partner, device_id_type=MESH,
        )

    def wide(h):
        return pl.ds(pl.multiple_of((hd * heads + h) * size, size), size)

    def band(peer):
        return pl.ds(pl.multiple_of(peer * share, share), share)

    order = (3, 1, 2, 0) if nh == 4 else tuple(range(nh - 1, -1, -1))

    def other(p):
        if nh != 4 or p == 0:
            return lax.rem(hd + p, nh)
        return (hd + 1 - 2 * lax.rem(hd, 2), lax.rem(hd + 2, 4), 3 - hd)[p - 1]

    def deal(h, p):
        peer = other(p)
        return pltpu.make_async_remote_copy(
            ob.at[h, band(peer)], out.at[0, :, wide(h)], a_s.at[0], a_r.at[p - 1],
            device_id=(peer, tok), device_id_type=MESH,
        )

    def keep(h):
        return pltpu.make_async_copy(ob.at[h, band(hd)], out.at[0, :, wide(h)], a_s.at[1])

    def deal_next(i, c, p):
        peer = other(p)
        return pltpu.make_async_remote_copy(
            ox.at[i, c * nh + peer], out.at[1, :, wide(mine(i))],
            b_s.at[i], b_p.at[i] if p == 0 else b_r.at[p - 1],
            device_id=(peer, 2 * z + c), device_id_type=MESH,
        )

    def keep_next(i):
        return pltpu.make_async_copy(
            ox.at[i, lane * nh + hd], out.at[1, :, wide(mine(i))], b_l.at[i]
        )

    def gradients(h, put, await_early=None, await_late=None):
        if await_early is not None:
            await_early()
        keys = kb[:, cut(h)]
        gate = wf[1, h].astype(BF)
        up = wf[2, h].astype(BF)
        wh[1, h] = gate
        wh[2, h] = up
        zg = mm(keys, gate)
        zu = mm(keys, up)
        sig = 1.0 / (1.0 + jnp.exp(-zg))
        silu = zg * sig
        hidden = (silu * zu).astype(BF)
        if await_late is not None:
            await_late()
        down = wf[0, h].astype(BF)
        wh[0, h] = down
        line = jnp.broadcast_to(rb[pl.ds(h, 1), :], (128, rows))
        column = jnp.transpose(line)
        column = jnp.concatenate([column] * (size // 128), axis=1)
        dout = (-(column * vb[:, cut(h)].astype(F32))).astype(BF)
        put(0, mm_tn(hidden, dout))
        dh = mm_nt(dout, down)
        dzu = (dh * silu).astype(BF)
        dzg = (dh * zu * sig * (1.0 + zg * (1.0 - sig))).astype(BF)
        put(1, mm_tn(keys, dzg))
        put(2, mm_tn(keys, dzu))

    def gradients_theirs(i, before=lambda k: None, waits=()):
        def put(k, part):
            sent[i, k] = part.astype(BF)
            before(k)
            if isinstance(i, int) and k == 0:
                for g in range(PIECES):
                    swap_piece(g).start()
            else:
                swap(i, k).start()

        gradients(theirs(i), put, *waits)

    def gradients_mine(i):
        def put(k, part):
            mg[k] = part

        gradients(mine(i), put)

    def add_first():
        for g in range(PIECES):
            part = pl.ds(g * piece, piece)
            swap_piece(g).wait_recv()
            own[0, part] = (mg[0, part] + got[0, 0, part].astype(F32)).astype(BF)

            @pl.when(last_end)
            def _():
                left(own, g).start()

            if g % PAIR == PAIR - 1:

                @pl.when(first_end)
                def _():
                    right(own, g // PAIR).start()

    def add_theirs(i):
        early = isinstance(i, int) and i == 0
        if early:
            add_first()
        begin = 1 if early else 0
        rest_of = got.at[i, pl.ds(begin, KINDS - begin)]
        pltpu.make_async_copy(rest_of, rest_of, sw_r.at[i]).wait()
        for k in range(begin, KINDS):
            own[KINDS * i + k] = (mg[k] + got[i, k].astype(F32)).astype(BF)

            @pl.when(first_end)
            def _():
                for g in range(PIECES // PAIR):
                    right(own, (KINDS * i + k) * (PIECES // PAIR) + g).start()

            @pl.when(last_end)
            def _():
                for g in range(PIECES):
                    left(own, per * i + k * PIECES + g).start()

    turn_at = per * (slots - 1)
    alone = (mine(slots - 1) < heads) & (theirs(slots - 1) >= heads)

    def turn(t, far):
        fast = (LAG_ALONE - LAG) * far
        held = jnp.where(t < turn_at + fast, -1, t - LAG_ALONE * far)
        return jnp.where(alone & (t >= turn_at), held, t - LAG * far)

    def pass_on(t):
        p = turn(t, z - 1)
        s = turn(t, nz - 2 - z)

        @pl.when(middle & (p >= 0) & (p < total) & (lax.rem(p, PAIR) == PAIR - 1))
        def _():
            n = p // PAIR
            m, part = place_right(n)
            right(po, n).wait_recv()
            po[m, part] = (pi[m, part].astype(F32) + own[m, part].astype(F32)).astype(BF)
            right(po, n).start()

        @pl.when(middle & (s >= 0) & (s < total))
        def _():
            m, part = place(s)
            left(so, s).wait_recv()
            so[m, part] = (si[m, part].astype(F32) + own[m, part].astype(F32)).astype(BF)
            left(so, s).start()

    def first(h):
        ob[h] = fast_apply(qb[:, cut(h)], wh[1, h], wh[2, h], wh[0, h])
        for p in order[:-1]:
            deal(h, p).start()
        keep(h).start()

    def gather_some(i, kinds):
        for k in kinds:
            m = KINDS * i + k

            @pl.when(first_end)
            def _():
                for g in range(PIECES):
                    left(own, per * i + k * PIECES + g).wait_recv()
                xs[k] = own[m].astype(F32) + si[m].astype(F32)

            @pl.when(last_end)
            def _():
                for g in range(PIECES // PAIR):
                    right(own, (KINDS * i + k) * (PIECES // PAIR) + g).wait_recv()
                xs[k] = own[m].astype(F32) + pi[m].astype(F32)

            @pl.when(middle)
            def _():
                xs[k] = own[m].astype(F32) + pi[m].astype(F32) + si[m].astype(F32)

        grads = [xs[k] for k in kinds]
        scales = [1.0 / (jnp.sqrt(jnp.sum(v * v)) + 1e-07) for v in grads]
        for k, v, scale in zip(kinds, grads, scales):
            xs[k] = v * scale

    def gather(i):
        gather_some(i, range(KINDS - 1))
        gather_some(i, [KINDS - 1])

    def sweep(i=None):
        x = [xs[k] for k in range(KINDS)]
        xb = [v.astype(BF) for v in x]
        gram = [mm_nt(v, v) for v in xb]
        half = [v.astype(BF) for v in gram]
        square = [mm(v, v) for v in half]
        poly = [(coef_second * a + coef_third * b).astype(BF) for a, b in zip(gram, square)]
        for k in range(KINDS):
            y = coef_first * x[k] + mm(poly[k], xb[k])
            if i is None:
                xs[k] = y
            else:
                wn[k] = (wf[k, mine(i)] - y).astype(BF)


    def second(i):
        x = qn[:, :, cut(mine(i))].reshape(2 * rows, size)
        ox[i] = fast_apply(x, wn[1], wn[2], wn[0]).reshape(2 * nh, share, size)
        for p in order:
            for c in range(2):
                if p > 0:
                    deal_next(i, c, p).start()
                else:

                    @pl.when(lane != c)
                    def _():
                        deal_next(i, c, p).start()

        keep_next(i).start()

    def ready_theirs(i):
        @pl.when(theirs(i) < heads)
        def _():
            gradients_theirs(i)

    def add_mine(i):
        @pl.when(mine(i) < heads)
        def _():
            add_theirs(i)

    def ready_mine(i):
        @pl.when((i < slots) & (mine(i) < heads))
        def _():
            gradients_mine(i)
            add_theirs(i)

    def first_of(h):
        @pl.when(h < heads)
        def _():
            first(h)

    first_loads = opening()
    for copy in first_loads:
        copy.start()
    greet_plane()
    load_head(1, cut(mine(0)), pl.ds(mine(0), 1))
    rest = heads - 2

    def early_waits():
        first_loads[0].wait()
        two = wf.at[pl.ds(1, 2), theirs(0)]
        pltpu.make_async_copy(two, two, ld.at[3, 1]).wait()

    def late_waits():
        for copy in first_loads[3:]:
            copy.wait()
        if rest > 0:
            load_head(2, pl.ds(2 * size, rest * size), pl.ds(2, rest))
        load_first.start()
        load_next.start()


    def enter(k):
        if k == 0:
            pl.semaphore_wait(barrier, 1 + 2 * (nh - 1) + inner)

    gradients_theirs(0, enter, (early_waits, late_waits))
    wait_head(1, 1)
    gradients_mine(0)
    add_theirs(0)
    if heads > 2:
        wait_head(2, rest)

        @pl.loop(1, slots)
        def _(i):
            ready_theirs(i)

    push_next.start()
    if slots > 1:

        @pl.when(mine(1) < heads)
        def _():
            gradients_mine(1)

    hops = max(nz - 3, 0)
    late = LAG * hops if turn_at - LAG * hops >= per * (slots - 2) else LAG_ALONE * hops
    behind, offset = late // per, late % per
    defer = middle & (mine(slots - 1) < heads)

    load_both.wait()

    @pl.loop(0, slots + behind)
    def _(r):
        base = per * r
        i = r - 1 - behind

        def done(work):
            def run():
                @pl.when((i >= 0) & jnp.logical_not(defer & (i == slots - 2)))
                def _():
                    work()

            return run

        def begin():
            @pl.when(i == 0)
            def _():
                push_next.wait_recv()

            gather(i)

        start = offset
        work = {1: [lambda: ready_mine(r + 2)]}
        firsts = (heads + 1) // 2
        for n in range(firsts):
            work[2 * n + 3] = [lambda n=n: first_of(firsts * r + n)]
        tail = []
        for n, item in enumerate([begin, None, sweep, sweep, None, lambda: sweep(i), lambda: second(i)]):
            if item is None:
                continue
            if start + n < per:
                work.setdefault(start + n, []).append(done(item))
            else:
                tail.append(done(item))
        for t in range(per):
            pass_on(base + t)
            if t == 0 and slots > 1:

                @pl.when(r == 0)
                def _():
                    add_mine(1)

            for item in work.get(t, []):
                item()
        for item in tail:
            item()

    @pl.loop(per * (slots + behind), per * slots + LAG_ALONE * hops)
    def _(t):
        pass_on(t)

    @pl.loop(jnp.where(defer, max(slots - 2, 0), slots - 1), slots)
    def _(i):
        @pl.when(mine(i) < heads)
        def _():
            if slots <= 2:

                @pl.when(i == 0)
                def _():
                        push_next.wait_recv()

            gather(i)
            for s in range(NS_STEPS):
                sweep(i if s == NS_STEPS - 1 else None)
            second(i)

    push_next.wait_send()

    @pl.loop(0, slots)
    def _(i):
        @pl.when(theirs(i) < heads)
        def _():
            pltpu.make_async_copy(sent.at[i], sent.at[i], sw_s.at[i]).wait()
            part = ox.at[i, 0]
            pltpu.make_async_copy(part, part, b_p.at[i]).wait()

        @pl.when(mine(i) < heads)
        def _():
            part = ox.at[i, pl.ds(0, 2 * nh - 1)]
            pltpu.make_async_copy(part, part, b_s.at[i]).wait()
            keep_next(i).wait()
            slot = own.at[pl.ds(KINDS * i, KINDS)]

            @pl.when(z < nz - 1)
            def _():
                pltpu.make_async_copy(slot, slot, p_s.at[i]).wait()

            @pl.when(z > 0)
            def _():
                pltpu.make_async_copy(slot, slot, s_s.at[i]).wait()

    part = ob.at[:, pl.ds(0, (nh - 1) * share)]
    pltpu.make_async_copy(part, part, a_s.at[0]).wait()
    part = ob.at[:, pl.ds(0, share)]
    pltpu.make_async_copy(part, part, a_s.at[1]).wait()
    for p in range(1, nh):
        part = out.at[0, :, pl.ds(0, heads * size)]
        pltpu.make_async_copy(part, part, a_r.at[p - 1]).wait()
        part = out.at[1, :, pl.ds(0, heads * size)]
        pltpu.make_async_copy(part, part, b_r.at[p - 1]).wait()


def solution(mesh):
    nh = mesh.shape["head"]
    nz = mesh.shape["tok"] // 2

    def local(queries, key_rows, value_rows, step_rates, gate_fast, up_fast, down_fast):
        heads, size, _ = gate_fast.shape
        rows = key_rows.shape[0]
        slots = (heads + 1) // 2
        matrices = KINDS * slots
        pieces = matrices * PIECES
        out_shape = (2, rows // nh, nh * heads * size)
        out_bytes = 2 * out_shape[0] * out_shape[1] * out_shape[2]
        anywhere = pl.BlockSpec(memory_space=pl.ANY)
        dma = pltpu.SemaphoreType.DMA
        stack = pltpu.VMEM((matrices, size, size), BF)
        return pl.pallas_call(
            functools.partial(kernel, nh, nz),
            out_shape=pltpu.VMEM(out_shape, BF),
            in_specs=[anywhere] * 7,
            out_specs=pl.BlockSpec(memory_space=pltpu.VMEM),
            scratch_shapes=[
                pltpu.VMEM((rows, heads * size), BF),
                pltpu.VMEM((2, rows, heads * size), BF),
                pltpu.VMEM((rows, heads * size), BF),
                pltpu.VMEM((rows, heads * size), BF),
                pltpu.VMEM((heads, rows), F32),
                pltpu.VMEM((KINDS, heads, size, size), F32),
                pltpu.VMEM((KINDS, heads, size, size), BF),
                stack,
                pltpu.VMEM((slots, KINDS, size, size), BF),
                pltpu.VMEM((slots, KINDS, size, size), BF),
                stack, stack, stack, stack,
                pltpu.VMEM((KINDS, size, size), F32),
                pltpu.VMEM((KINDS, size, size), F32),
                pltpu.VMEM((KINDS, size, size), BF),
                pltpu.VMEM((heads, rows, size), BF),
                pltpu.VMEM((slots, 2 * nh, rows // nh, size), BF),
                dma((5, 2)),
                dma((2,)),
                dma((slots,)), dma((PIECES,)), dma((slots,)),
                dma((slots,)), dma((pieces // PAIR,)),
                dma((slots,)), dma((pieces,)),
                dma((2,)), dma((nh - 1,)),
                dma((slots,)), dma((nh - 1,)), dma((slots,)), dma((slots,)),
            ],
            compiler_params=pltpu.CompilerParams(
                collective_id=0,
                has_side_effects=True,
                vmem_limit_bytes=VMEM_BYTES - out_bytes - 16384,
            ),
        )(queries, key_rows, value_rows, step_rates, gate_fast, up_fast, down_fast)

    placed = (
        P(None, "tok", "head"),
        P("tok", "head"),
        P("tok", "head"),
        P("head", "tok"),
        P("head", None, None),
        P("head", None, None),
        P("head", None, None),
    )
    return jax.shard_map(
        local, mesh=mesh, in_specs=placed, out_specs=P(None, ("tok", "head"), None), check_vma=False
    )
```

```python
import functools

import jax
import jax.numpy as jnp
from jax import lax
from jax.experimental import pallas as pl
from jax.experimental.pallas import tpu as pltpu
from jax.sharding import PartitionSpec as P

NS_STEPS = 3
KINDS = 3
PIECES = 4
PAIR = 2
LAG = 5
LAG_ALONE = 9
VMEM_BYTES = 67043328

coef_first = 3.4445
coef_second = -4.775
coef_third = 2.0315

MESH = pl.DeviceIdType.MESH
BF = jnp.bfloat16
F32 = jnp.float32


def mm(a, b):
    return jnp.dot(a, b, preferred_element_type=F32)


def mm_tn(a, b):
    return lax.dot_general(a, b, (((0,), (0,)), ((), ())), preferred_element_type=F32)


def mm_nt(a, b):
    return lax.dot_general(a, b, (((1,), (1,)), ((), ())), preferred_element_type=F32)


def fast_apply(x, gate, up, down):
    pre = mm(x, gate)
    hidden = (pre / (1.0 + jnp.exp(-pre)) * mm(x, up)).astype(BF)
    return mm(hidden, down).astype(BF)


def kernel(
    nh, nz, q_in, k_in, v_in, r_in, g_in, u_in, d_in, out,
    qb, qn, kb, vb, rb, wf, wh, own, sent, got, pi, si, po, so, mg, xs, wn, ob, ox,
    a_s, a_r, b_s, b_r, b_p, b_l,
):
    heads, share, size = ob.shape[0], ob.shape[1] // nh, ob.shape[2]
    rows = nh * share
    slots = sent.shape[0]
    piece = size // PIECES
    per = KINDS * PIECES
    hd = lax.axis_index("head")
    tok = lax.axis_index("tok")
    lane = lax.rem(tok, 2)
    z = tok // 2
    partner = (hd, z * 2 + 1 - lane)
    total = per * ((heads + 1 - lane) // 2)
    first_end = z == 0
    last_end = z == nz - 1
    middle = jnp.logical_not(first_end) & jnp.logical_not(last_end)

    def cut(h):
        return pl.ds(h * size if isinstance(h, int) else pl.multiple_of(h * size, size), size)

    def mine(i):
        return 2 * i + lane

    def theirs(i):
        return 2 * i + 1 - lane

    def main(ld, qs, sw_s, sw_p, sw_r, p_s, p_r, s_s, s_r):
        barrier = pltpu.get_barrier_semaphore()

        inner = (z > 0).astype(jnp.int32) + (z < nz - 1).astype(jnp.int32)

        def greet_plane():
            pl.semaphore_signal(barrier, inc=1, device_id=partner, device_id_type=MESH)
            for p in range(1, nh):
                for c in range(2):
                    pl.semaphore_signal(
                        barrier, inc=1, device_id=(lax.rem(hd + p, nh), 2 * z + c), device_id_type=MESH
                    )

        def load_head(stage, columns, some):
            pltpu.make_async_copy(k_in.at[:, columns], kb.at[:, columns], ld.at[stage, 0]).start()
            for k, src in ((1, g_in), (2, u_in)):
                pltpu.make_async_copy(src.at[some], wf.at[k, some], ld.at[stage, 1]).start()
            pltpu.make_async_copy(v_in.at[:, columns], vb.at[:, columns], ld.at[stage, 0]).start()
            pltpu.make_async_copy(d_in.at[some], wf.at[0, some], ld.at[stage, 1]).start()

        def wait_head(stage, count):
            both = q_in.at[:, :, pl.ds(0, count * size)]
            pltpu.make_async_copy(both, both, ld.at[stage, 0]).wait()
            three = wf.at[:, pl.ds(0, count)]
            pltpu.make_async_copy(three, three, ld.at[stage, 1]).wait()

        def opening():
            h = theirs(0)
            some = pl.ds(h, 1)
            keys = pltpu.make_async_copy(k_in.at[:, cut(h)], kb.at[:, cut(h)], ld.at[0, 0])
            values = pltpu.make_async_copy(v_in.at[:, cut(h)], vb.at[:, cut(h)], ld.at[0, 1])
            gates = pltpu.make_async_copy(g_in.at[some], wf.at[1, some], ld.at[3, 1])
            ups = pltpu.make_async_copy(u_in.at[some], wf.at[2, some], ld.at[3, 1])
            downs = pltpu.make_async_copy(d_in.at[some], wf.at[0, some], ld.at[4, 1])
            return keys, gates, ups, values, downs, load_rates

        load_rates = pltpu.make_async_copy(r_in, rb, ld.at[3, 0])
        load_first = pltpu.make_async_copy(q_in.at[0], qb, ld.at[4, 0])
        load_next = pltpu.make_async_copy(q_in.at[1], qn.at[lane], ld.at[4, 0])
        load_both = pltpu.make_async_copy(q_in, q_in, ld.at[4, 0])
        push_next = pltpu.make_async_remote_copy(
            q_in.at[1], qn.at[lane], qs.at[0], qs.at[1], device_id=partner, device_id_type=MESH
        )

        def place(t):
            return t // PIECES, pl.ds(pl.multiple_of(lax.rem(t, PIECES) * piece, piece), piece)

        def place_right(t):
            span = PAIR * piece
            each = PIECES // PAIR
            return t // each, pl.ds(pl.multiple_of(lax.rem(t, each) * span, span), span)

        def right(src, t):
            m, part = place_right(t)
            return pltpu.make_async_remote_copy(
                src.at[m, part], pi.at[m, part], p_s.at[t // (per // PAIR)], p_r.at[t],
                device_id=(hd, tok + 2), device_id_type=MESH,
            )

        def left(src, t):
            m, part = place(t)
            return pltpu.make_async_remote_copy(
                src.at[m, part], si.at[m, part], s_s.at[t // per], s_r.at[t],
                device_id=(hd, tok - 2), device_id_type=MESH,
            )

        def swap(i, k):
            return pltpu.make_async_remote_copy(
                sent.at[i, k], got.at[i, k], sw_s.at[i], sw_r.at[i],
                device_id=partner, device_id_type=MESH,
            )

        def swap_piece(g):
            part = pl.ds(g * piece, piece)
            return pltpu.make_async_remote_copy(
                sent.at[0, 0, part], got.at[0, 0, part], sw_s.at[0], sw_p.at[g],
                device_id=partner, device_id_type=MESH,
            )

        def wide(h):
            return pl.ds(pl.multiple_of((hd * heads + h) * size, size), size)

        def band(peer):
            return pl.ds(pl.multiple_of(peer * share, share), share)

        order = (3, 1, 2, 0) if nh == 4 else tuple(range(nh - 1, -1, -1))

        def other(p):
            if nh != 4 or p == 0:
                return lax.rem(hd + p, nh)
            return (hd + 1 - 2 * lax.rem(hd, 2), lax.rem(hd + 2, 4), 3 - hd)[p - 1]

        def deal(h, p):
            peer = other(p)
            return pltpu.make_async_remote_copy(
                ob.at[h, band(peer)], out.at[0, :, wide(h)], a_s.at[0], a_r.at[p - 1],
                device_id=(peer, tok), device_id_type=MESH,
            )

        def keep(h):
            return pltpu.make_async_copy(ob.at[h, band(hd)], out.at[0, :, wide(h)], a_s.at[1])

        def deal_next(i, c, p):
            peer = other(p)
            return pltpu.make_async_remote_copy(
                ox.at[i, c * nh + peer], out.at[1, :, wide(mine(i))],
                b_s.at[i], b_p.at[i] if p == 0 else b_r.at[p - 1],
                device_id=(peer, 2 * z + c), device_id_type=MESH,
            )

        def keep_next(i):
            return pltpu.make_async_copy(
                ox.at[i, lane * nh + hd], out.at[1, :, wide(mine(i))], b_l.at[i]
            )

        def gradients(h, put, await_early=None, await_late=None):
            if await_early is not None:
                await_early()
            keys = kb[:, cut(h)]
            gate = wf[1, h].astype(BF)
            up = wf[2, h].astype(BF)
            wh[1, h] = gate
            wh[2, h] = up
            zg = mm(keys, gate)
            zu = mm(keys, up)
            sig = 1.0 / (1.0 + jnp.exp(-zg))
            silu = zg * sig
            hidden = (silu * zu).astype(BF)
            if await_late is not None:
                await_late()
            down = wf[0, h].astype(BF)
            wh[0, h] = down
            line = jnp.broadcast_to(rb[pl.ds(h, 1), :], (128, rows))
            column = jnp.transpose(line)
            column = jnp.concatenate([column] * (size // 128), axis=1)
            dout = (-(column * vb[:, cut(h)].astype(F32))).astype(BF)
            put(0, mm_tn(hidden, dout))
            dh = mm_nt(dout, down)
            dzu = (dh * silu).astype(BF)
            dzg = (dh * zu * sig * (1.0 + zg * (1.0 - sig))).astype(BF)
            put(1, mm_tn(keys, dzg))
            put(2, mm_tn(keys, dzu))

        def gradients_theirs(i, before=lambda k: None, waits=()):
            def put(k, part):
                sent[i, k] = part.astype(BF)
                before(k)
                if isinstance(i, int) and k == 0:
                    for g in range(PIECES):
                        swap_piece(g).start()
                else:
                    swap(i, k).start()

            gradients(theirs(i), put, *waits)

        def gradients_mine(i):
            def put(k, part):
                mg[k] = part

            gradients(mine(i), put)

        def add_first():
            for g in range(PIECES):
                part = pl.ds(g * piece, piece)
                swap_piece(g).wait_recv()
                own[0, part] = (mg[0, part] + got[0, 0, part].astype(F32)).astype(BF)

                @pl.when(last_end)
                def _():
                    left(own, g).start()

                if g % PAIR == PAIR - 1:

                    @pl.when(first_end)
                    def _():
                        right(own, g // PAIR).start()

        def add_theirs(i):
            early = isinstance(i, int) and i == 0
            if early:
                add_first()
            begin = 1 if early else 0
            rest_of = got.at[i, pl.ds(begin, KINDS - begin)]
            pltpu.make_async_copy(rest_of, rest_of, sw_r.at[i]).wait()
            for k in range(begin, KINDS):
                own[KINDS * i + k] = (mg[k] + got[i, k].astype(F32)).astype(BF)

                @pl.when(first_end)
                def _():
                    for g in range(PIECES // PAIR):
                        right(own, (KINDS * i + k) * (PIECES // PAIR) + g).start()

                @pl.when(last_end)
                def _():
                    for g in range(PIECES):
                        left(own, per * i + k * PIECES + g).start()

        turn_at = per * (slots - 1)
        alone = (mine(slots - 1) < heads) & (theirs(slots - 1) >= heads)

        def turn(t, far):
            fast = (LAG_ALONE - LAG) * far
            held = jnp.where(t < turn_at + fast, -1, t - LAG_ALONE * far)
            return jnp.where(alone & (t >= turn_at), held, t - LAG * far)

        def pass_on(t):
            p = turn(t, z - 1)
            s = turn(t, nz - 2 - z)

            @pl.when(middle & (p >= 0) & (p < total) & (lax.rem(p, PAIR) == PAIR - 1))
            def _():
                n = p // PAIR
                m, part = place_right(n)
                right(po, n).wait_recv()
                po[m, part] = (pi[m, part].astype(F32) + own[m, part].astype(F32)).astype(BF)
                right(po, n).start()

            @pl.when(middle & (s >= 0) & (s < total))
            def _():
                m, part = place(s)
                left(so, s).wait_recv()
                so[m, part] = (si[m, part].astype(F32) + own[m, part].astype(F32)).astype(BF)
                left(so, s).start()

        def first(h):
            ob[h] = fast_apply(qb[:, cut(h)], wh[1, h], wh[2, h], wh[0, h])
            for p in order[:-1]:
                deal(h, p).start()
            keep(h).start()

        def gather_some(i, kinds):
            for k in kinds:
                m = KINDS * i + k

                @pl.when(first_end)
                def _():
                    for g in range(PIECES):
                        left(own, per * i + k * PIECES + g).wait_recv()
                    xs[k] = own[m].astype(F32) + si[m].astype(F32)

                @pl.when(last_end)
                def _():
                    for g in range(PIECES // PAIR):
                        right(own, (KINDS * i + k) * (PIECES // PAIR) + g).wait_recv()
                    xs[k] = own[m].astype(F32) + pi[m].astype(F32)

                @pl.when(middle)
                def _():
                    xs[k] = own[m].astype(F32) + pi[m].astype(F32) + si[m].astype(F32)

            grads = [xs[k] for k in kinds]
            scales = [1.0 / (jnp.sqrt(jnp.sum(v * v)) + 1e-07) for v in grads]
            for k, v, scale in zip(kinds, grads, scales):
                xs[k] = v * scale

        def gather(i):
            gather_some(i, range(KINDS - 1))
            gather_some(i, [KINDS - 1])

        def sweep(i=None):
            x = [xs[k] for k in range(KINDS)]
            xb = [v.astype(BF) for v in x]
            gram = [mm_nt(v, v) for v in xb]
            half = [v.astype(BF) for v in gram]
            square = [mm(v, v) for v in half]
            poly = [(coef_second * a + coef_third * b).astype(BF) for a, b in zip(gram, square)]
            for k in range(KINDS):
                y = coef_first * x[k] + mm(poly[k], xb[k])
                if i is None:
                    xs[k] = y
                else:
                    wn[k] = (wf[k, mine(i)] - y).astype(BF)


        def second(i):
            x = qn[:, :, cut(mine(i))].reshape(2 * rows, size)
            ox[i] = fast_apply(x, wn[1], wn[2], wn[0]).reshape(2 * nh, share, size)
            for p in order:
                for c in range(2):
                    if p > 0:
                        deal_next(i, c, p).start()
                    else:

                        @pl.when(lane != c)
                        def _():
                            deal_next(i, c, p).start()

            keep_next(i).start()

        def ready_theirs(i):
            @pl.when(theirs(i) < heads)
            def _():
                gradients_theirs(i)

        def add_mine(i):
            @pl.when(mine(i) < heads)
            def _():
                add_theirs(i)

        def ready_mine(i):
            @pl.when((i < slots) & (mine(i) < heads))
            def _():
                gradients_mine(i)
                add_theirs(i)

        def first_of(h):
            @pl.when(h < heads)
            def _():
                first(h)

        first_loads = opening()
        for copy in first_loads:
            copy.start()

        @pl.when(z > 0)
        def _():
            pl.semaphore_signal(barrier, inc=1, device_id=(hd, tok - 2), device_id_type=MESH)

        @pl.when(z < nz - 1)
        def _():
            pl.semaphore_signal(barrier, inc=1, device_id=(hd, tok + 2), device_id_type=MESH)

        greet_plane()
        load_head(1, cut(mine(0)), pl.ds(mine(0), 1))
        rest = heads - 2

        def early_waits():
            first_loads[0].wait()
            two = wf.at[pl.ds(1, 2), theirs(0)]
            pltpu.make_async_copy(two, two, ld.at[3, 1]).wait()

        def late_waits():
            for copy in first_loads[3:]:
                copy.wait()
            if rest > 0:
                load_head(2, pl.ds(2 * size, rest * size), pl.ds(2, rest))
            load_first.start()
            load_next.start()


        def enter(k):
            if k == 0:
                pl.semaphore_wait(barrier, 1 + 2 * (nh - 1) + inner)

        gradients_theirs(0, enter, (early_waits, late_waits))
        wait_head(1, 1)
        gradients_mine(0)
        add_theirs(0)
        if heads > 2:
            wait_head(2, rest)

            @pl.loop(1, slots)
            def _(i):
                ready_theirs(i)

        push_next.start()
        if slots > 1:

            @pl.when(mine(1) < heads)
            def _():
                gradients_mine(1)

        hops = max(nz - 3, 0)
        late = LAG * hops if turn_at - LAG * hops >= per * (slots - 2) else LAG_ALONE * hops
        behind, offset = late // per, late % per
        defer = middle & (mine(slots - 1) < heads)

        load_both.wait()

        @pl.loop(0, slots + behind)
        def _(r):
            base = per * r
            i = r - 1 - behind

            def done(work):
                def run():
                    @pl.when((i >= 0) & jnp.logical_not(defer & (i == slots - 2)))
                    def _():
                        work()

                return run

            def begin():
                @pl.when(i == 0)
                def _():
                    push_next.wait_recv()

                gather(i)

            start = offset
            work = {1: [lambda: ready_mine(r + 2)]}
            firsts = (heads + 1) // 2
            for n in range(firsts):
                work[2 * n + 3] = [lambda n=n: first_of(firsts * r + n)]
            tail = []
            for n, item in enumerate([begin, None, sweep, sweep, None, lambda: sweep(i), lambda: second(i)]):
                if item is None:
                    continue
                if start + n < per:
                    work.setdefault(start + n, []).append(done(item))
                else:
                    tail.append(done(item))
            for t in range(per):
                pass_on(base + t)
                if t == 0 and slots > 1:

                    @pl.when(r == 0)
                    def _():
                        add_mine(1)

                for item in work.get(t, []):
                    item()
            for item in tail:
                item()

        @pl.loop(per * (slots + behind), per * slots + LAG_ALONE * hops)
        def _(t):
            pass_on(t)

        @pl.loop(jnp.where(defer, max(slots - 2, 0), slots - 1), slots)
        def _(i):
            @pl.when(mine(i) < heads)
            def _():
                if slots <= 2:

                    @pl.when(i == 0)
                    def _():
                            push_next.wait_recv()

                gather(i)
                for s in range(NS_STEPS):
                    sweep(i if s == NS_STEPS - 1 else None)
                second(i)

        push_next.wait_send()

        @pl.loop(0, slots)
        def _(i):
            @pl.when(theirs(i) < heads)
            def _():
                pltpu.make_async_copy(sent.at[i], sent.at[i], sw_s.at[i]).wait()

            @pl.when(mine(i) < heads)
            def _():
                slot = own.at[pl.ds(KINDS * i, KINDS)]

                @pl.when(z < nz - 1)
                def _():
                    pltpu.make_async_copy(slot, slot, p_s.at[i]).wait()

                @pl.when(z > 0)
                def _():
                    pltpu.make_async_copy(slot, slot, s_s.at[i]).wait()

    dma = pltpu.SemaphoreType.DMA
    pieces = KINDS * slots * PIECES
    pl.run_scoped(
        main,
        dma((5, 2)), dma((2,)),
        dma((slots,)), dma((PIECES,)), dma((slots,)),
        dma((slots,)), dma((pieces // PAIR,)),
        dma((slots,)), dma((pieces,)),
    )

    @pl.loop(0, slots)
    def _(i):
        part = ox.at[i, 0]

        @pl.when(theirs(i) < heads)
        def _():
            pltpu.make_async_copy(part, part, b_p.at[i]).wait()

        @pl.when(mine(i) < heads)
        def _():
            most = ox.at[i, pl.ds(0, 2 * nh - 1)]
            pltpu.make_async_copy(most, most, b_s.at[i]).wait()
            pltpu.make_async_copy(part, part, b_l.at[i]).wait()

    part = ob.at[:, pl.ds(0, (nh - 1) * share)]
    pltpu.make_async_copy(part, part, a_s.at[0]).wait()
    part = ob.at[:, pl.ds(0, share)]
    pltpu.make_async_copy(part, part, a_s.at[1]).wait()
    for p in range(1, nh):
        part = out.at[0, :, pl.ds(0, heads * size)]
        pltpu.make_async_copy(part, part, a_r.at[p - 1]).wait()
        part = out.at[1, :, pl.ds(0, heads * size)]
        pltpu.make_async_copy(part, part, b_r.at[p - 1]).wait()


def solution(mesh):
    nh = mesh.shape["head"]
    nz = mesh.shape["tok"] // 2

    def local(queries, key_rows, value_rows, step_rates, gate_fast, up_fast, down_fast):
        heads, size, _ = gate_fast.shape
        rows = key_rows.shape[0]
        slots = (heads + 1) // 2
        matrices = KINDS * slots
        out_shape = (2, rows // nh, nh * heads * size)
        out_bytes = 2 * out_shape[0] * out_shape[1] * out_shape[2]
        anywhere = pl.BlockSpec(memory_space=pl.ANY)
        dma = pltpu.SemaphoreType.DMA
        stack = pltpu.VMEM((matrices, size, size), BF)
        return pl.pallas_call(
            functools.partial(kernel, nh, nz),
            out_shape=pltpu.VMEM(out_shape, BF),
            in_specs=[anywhere] * 7,
            out_specs=pl.BlockSpec(memory_space=pltpu.VMEM),
            scratch_shapes=[
                pltpu.VMEM((rows, heads * size), BF),
                pltpu.VMEM((2, rows, heads * size), BF),
                pltpu.VMEM((rows, heads * size), BF),
                pltpu.VMEM((rows, heads * size), BF),
                pltpu.VMEM((heads, rows), F32),
                pltpu.VMEM((KINDS, heads, size, size), F32),
                pltpu.VMEM((KINDS, heads, size, size), BF),
                stack,
                pltpu.VMEM((slots, KINDS, size, size), BF),
                pltpu.VMEM((slots, KINDS, size, size), BF),
                stack, stack, stack, stack,
                pltpu.VMEM((KINDS, size, size), F32),
                pltpu.VMEM((KINDS, size, size), F32),
                pltpu.VMEM((KINDS, size, size), BF),
                pltpu.VMEM((heads, rows, size), BF),
                pltpu.VMEM((slots, 2 * nh, rows // nh, size), BF),
                dma((2,)), dma((nh - 1,)),
                dma((slots,)), dma((nh - 1,)), dma((slots,)), dma((slots,)),
            ],
            compiler_params=pltpu.CompilerParams(
                collective_id=0,
                has_side_effects=True,
                vmem_limit_bytes=VMEM_BYTES - out_bytes - 16384,
            ),
        )(queries, key_rows, value_rows, step_rates, gate_fast, up_fast, down_fast)

    placed = (
        P(None, "tok", "head"),
        P("tok", "head"),
        P("tok", "head"),
        P("head", "tok"),
        P("head", None, None),
        P("head", None, None),
        P("head", None, None),
    )
    return jax.shard_map(
        local, mesh=mesh, in_specs=placed, out_specs=P(None, ("tok", "head"), None), check_vma=False
    )
```

```python
import functools

import jax
import jax.numpy as jnp
from jax import lax
from jax.experimental import pallas as pl
from jax.experimental.pallas import tpu as pltpu
from jax.sharding import PartitionSpec as P

NS_STEPS = 3
KINDS = 3
PIECES = 8
PAIR = 2
LAG = 10
LAG_ALONE = 18
VMEM_BYTES = 67043328

coef_first = 3.4445
coef_second = -4.775
coef_third = 2.0315

MESH = pl.DeviceIdType.MESH
BF = jnp.bfloat16
F32 = jnp.float32


def mm(a, b):
    return jnp.dot(a, b, preferred_element_type=F32)


def mm_tn(a, b):
    return lax.dot_general(a, b, (((0,), (0,)), ((), ())), preferred_element_type=F32)


def mm_nt(a, b):
    return lax.dot_general(a, b, (((1,), (1,)), ((), ())), preferred_element_type=F32)


def fast_apply(x, gate, up, down):
    pre = mm(x, gate)
    hidden = (pre / (1.0 + jnp.exp(-pre)) * mm(x, up)).astype(BF)
    return mm(hidden, down).astype(BF)


def kernel(
    nh, nz, q_in, k_in, v_in, r_in, g_in, u_in, d_in, out,
    qb, qn, kb, vb, rb, wf, wh, own, sent, got, pi, si, po, so, mg, xs, wn, ob, ox,
):
    heads, share, size = ob.shape[0], ob.shape[1] // nh, ob.shape[2]
    rows = nh * share
    slots = sent.shape[0]
    piece = size // PIECES
    per = KINDS * PIECES
    hd = lax.axis_index("head")
    tok = lax.axis_index("tok")
    lane = lax.rem(tok, 2)
    z = tok // 2
    partner = (hd, z * 2 + 1 - lane)
    total = per * ((heads + 1 - lane) // 2)
    first_end = z == 0
    last_end = z == nz - 1
    middle = jnp.logical_not(first_end) & jnp.logical_not(last_end)

    def cut(h):
        return pl.ds(h * size if isinstance(h, int) else pl.multiple_of(h * size, size), size)

    def mine(i):
        return 2 * i + lane

    def theirs(i):
        return 2 * i + 1 - lane

    def main(ld, qs, sw_s, sw_p, sw_r, p_s, p_r, s_s, s_r, a_s, a_r, b_s, b_r, b_p, b_l):
        barrier = pltpu.get_barrier_semaphore()

        inner = (z > 0).astype(jnp.int32) + (z < nz - 1).astype(jnp.int32)

        def greet_plane():
            pl.semaphore_signal(barrier, inc=1, device_id=partner, device_id_type=MESH)
            for p in range(1, nh):
                for c in range(2):
                    pl.semaphore_signal(
                        barrier, inc=1, device_id=(lax.rem(hd + p, nh), 2 * z + c), device_id_type=MESH
                    )

        def load_head(stage, columns, some):
            pltpu.make_async_copy(k_in.at[:, columns], kb.at[:, columns], ld.at[stage, 0]).start()
            for k, src in ((1, g_in), (2, u_in)):
                pltpu.make_async_copy(src.at[some], wf.at[k, some], ld.at[stage, 1]).start()
            pltpu.make_async_copy(v_in.at[:, columns], vb.at[:, columns], ld.at[stage, 0]).start()
            pltpu.make_async_copy(d_in.at[some], wf.at[0, some], ld.at[stage, 1]).start()

        def wait_head(stage, count):
            both = q_in.at[:, :, pl.ds(0, count * size)]
            pltpu.make_async_copy(both, both, ld.at[stage, 0]).wait()
            three = wf.at[:, pl.ds(0, count)]
            pltpu.make_async_copy(three, three, ld.at[stage, 1]).wait()

        def opening():
            h = theirs(0)
            some = pl.ds(h, 1)
            keys = pltpu.make_async_copy(k_in.at[:, cut(h)], kb.at[:, cut(h)], ld.at[0, 0])
            values = pltpu.make_async_copy(v_in.at[:, cut(h)], vb.at[:, cut(h)], ld.at[0, 1])
            gates = pltpu.make_async_copy(g_in.at[some], wf.at[1, some], ld.at[3, 1])
            ups = pltpu.make_async_copy(u_in.at[some], wf.at[2, some], ld.at[3, 1])
            downs = pltpu.make_async_copy(d_in.at[some], wf.at[0, some], ld.at[4, 1])
            return keys, gates, ups, values, downs, load_rates

        load_rates = pltpu.make_async_copy(r_in, rb, ld.at[3, 0])
        load_first = pltpu.make_async_copy(q_in.at[0], qb, ld.at[4, 0])
        load_next = pltpu.make_async_copy(q_in.at[1], qn.at[lane], ld.at[4, 0])
        load_both = pltpu.make_async_copy(q_in, q_in, ld.at[4, 0])
        push_next = pltpu.make_async_remote_copy(
            q_in.at[1], qn.at[lane], qs.at[0], qs.at[1], device_id=partner, device_id_type=MESH
        )

        def place(t):
            return t // PIECES, pl.ds(pl.multiple_of(lax.rem(t, PIECES) * piece, piece), piece)

        def place_right(t):
            span = PAIR * piece
            each = PIECES // PAIR
            return t // each, pl.ds(pl.multiple_of(lax.rem(t, each) * span, span), span)

        def right(src, t):
            m, part = place_right(t)
            return pltpu.make_async_remote_copy(
                src.at[m, part], pi.at[m, part], p_s.at[t // (per // PAIR)], p_r.at[t],
                device_id=(hd, tok + 2), device_id_type=MESH,
            )

        def left(src, t):
            m, part = place(t)
            return pltpu.make_async_remote_copy(
                src.at[m, part], si.at[m, part], s_s.at[t // per], s_r.at[t],
                device_id=(hd, tok - 2), device_id_type=MESH,
            )

        def swap(i, k):
            return pltpu.make_async_remote_copy(
                sent.at[i, k], got.at[i, k], sw_s.at[i], sw_r.at[i],
                device_id=partner, device_id_type=MESH,
            )

        def swap_piece(g):
            part = pl.ds(g * piece, piece)
            return pltpu.make_async_remote_copy(
                sent.at[0, 0, part], got.at[0, 0, part], sw_s.at[0], sw_p.at[g],
                device_id=partner, device_id_type=MESH,
            )

        def wide(h):
            return pl.ds(pl.multiple_of((hd * heads + h) * size, size), size)

        def band(peer):
            return pl.ds(pl.multiple_of(peer * share, share), share)

        order = (3, 1, 2, 0) if nh == 4 else tuple(range(nh - 1, -1, -1))

        def other(p):
            if nh != 4 or p == 0:
                return lax.rem(hd + p, nh)
            return (hd + 1 - 2 * lax.rem(hd, 2), lax.rem(hd + 2, 4), 3 - hd)[p - 1]

        def deal(h, p):
            peer = other(p)
            return pltpu.make_async_remote_copy(
                ob.at[h, band(peer)], out.at[0, :, wide(h)], a_s.at[0], a_r.at[p - 1],
                device_id=(peer, tok), device_id_type=MESH,
            )

        def keep(h):
            return pltpu.make_async_copy(ob.at[h, band(hd)], out.at[0, :, wide(h)], a_s.at[1])

        def deal_next(i, c, p):
            peer = other(p)
            return pltpu.make_async_remote_copy(
                ox.at[i, c * nh + peer], out.at[1, :, wide(mine(i))],
                b_s.at[i], b_p.at[i] if p == 0 else b_r.at[p - 1],
                device_id=(peer, 2 * z + c), device_id_type=MESH,
            )

        def keep_next(i):
            return pltpu.make_async_copy(
                ox.at[i, lane * nh + hd], out.at[1, :, wide(mine(i))], b_l.at[i]
            )

        def gradients(h, put, await_early=None, await_late=None):
            if await_early is not None:
                await_early()
            keys = kb[:, cut(h)]
            gate = wf[1, h].astype(BF)
            up = wf[2, h].astype(BF)
            wh[1, h] = gate
            wh[2, h] = up
            zg = mm(keys, gate)
            zu = mm(keys, up)
            sig = 1.0 / (1.0 + jnp.exp(-zg))
            silu = zg * sig
            hidden = (silu * zu).astype(BF)
            if await_late is not None:
                await_late()
            down = wf[0, h].astype(BF)
            wh[0, h] = down
            line = jnp.broadcast_to(rb[pl.ds(h, 1), :], (128, rows))
            column = jnp.transpose(line)
            column = jnp.concatenate([column] * (size // 128), axis=1)
            dout = (-(column * vb[:, cut(h)].astype(F32))).astype(BF)
            put(0, mm_tn(hidden, dout))
            dh = mm_nt(dout, down)
            dzu = (dh * silu).astype(BF)
            dzg = (dh * zu * sig * (1.0 + zg * (1.0 - sig))).astype(BF)
            put(1, mm_tn(keys, dzg))
            put(2, mm_tn(keys, dzu))

        def gradients_theirs(i, before=lambda k: None, waits=()):
            def put(k, part):
                sent[i, k] = part.astype(BF)
                before(k)
                if isinstance(i, int) and k == 0:
                    for g in range(PIECES):
                        swap_piece(g).start()
                else:
                    swap(i, k).start()

            gradients(theirs(i), put, *waits)

        def gradients_mine(i):
            def put(k, part):
                mg[k] = part

            gradients(mine(i), put)

        def add_first():
            for g in range(PIECES):
                part = pl.ds(g * piece, piece)
                swap_piece(g).wait_recv()
                own[0, part] = (mg[0, part] + got[0, 0, part].astype(F32)).astype(BF)

                @pl.when(last_end)
                def _():
                    left(own, g).start()

                if g % PAIR == PAIR - 1:

                    @pl.when(first_end)
                    def _():
                        right(own, g // PAIR).start()

        def add_theirs(i):
            early = isinstance(i, int) and i == 0
            if early:
                add_first()
            begin = 1 if early else 0
            rest_of = got.at[i, pl.ds(begin, KINDS - begin)]
            pltpu.make_async_copy(rest_of, rest_of, sw_r.at[i]).wait()
            for k in range(begin, KINDS):
                own[KINDS * i + k] = (mg[k] + got[i, k].astype(F32)).astype(BF)

                @pl.when(first_end)
                def _():
                    for g in range(PIECES // PAIR):
                        right(own, (KINDS * i + k) * (PIECES // PAIR) + g).start()

                @pl.when(last_end)
                def _():
                    for g in range(PIECES):
                        left(own, per * i + k * PIECES + g).start()

        turn_at = per * (slots - 1)
        alone = (mine(slots - 1) < heads) & (theirs(slots - 1) >= heads)

        def turn(t, far):
            fast = (LAG_ALONE - LAG) * far
            held = jnp.where(t < turn_at + fast, -1, t - LAG_ALONE * far)
            return jnp.where(alone & (t >= turn_at), held, t - LAG * far)

        def pass_on(t):
            p = turn(t, z - 1)
            s = turn(t, nz - 2 - z)

            @pl.when(middle & (p >= 0) & (p < total) & (lax.rem(p, PAIR) == PAIR - 1))
            def _():
                n = p // PAIR
                m, part = place_right(n)
                right(po, n).wait_recv()
                po[m, part] = (pi[m, part].astype(F32) + own[m, part].astype(F32)).astype(BF)
                right(po, n).start()

            @pl.when(middle & (s >= 0) & (s < total))
            def _():
                m, part = place(s)
                left(so, s).wait_recv()
                so[m, part] = (si[m, part].astype(F32) + own[m, part].astype(F32)).astype(BF)
                left(so, s).start()

        def first(h):
            ob[h] = fast_apply(qb[:, cut(h)], wh[1, h], wh[2, h], wh[0, h])
            for p in order[:-1]:
                deal(h, p).start()
            keep(h).start()

        def gather_some(i, kinds):
            for k in kinds:
                m = KINDS * i + k

                @pl.when(first_end)
                def _():
                    for g in range(PIECES):
                        left(own, per * i + k * PIECES + g).wait_recv()
                    xs[k] = own[m].astype(F32) + si[m].astype(F32)

                @pl.when(last_end)
                def _():
                    for g in range(PIECES // PAIR):
                        right(own, (KINDS * i + k) * (PIECES // PAIR) + g).wait_recv()
                    xs[k] = own[m].astype(F32) + pi[m].astype(F32)

                @pl.when(middle)
                def _():
                    xs[k] = own[m].astype(F32) + pi[m].astype(F32) + si[m].astype(F32)

            grads = [xs[k] for k in kinds]
            scales = [1.0 / (jnp.sqrt(jnp.sum(v * v)) + 1e-07) for v in grads]
            for k, v, scale in zip(kinds, grads, scales):
                xs[k] = v * scale

        def gather(i):
            gather_some(i, range(KINDS - 1))
            gather_some(i, [KINDS - 1])

        def sweep(i=None):
            x = [xs[k] for k in range(KINDS)]
            xb = [v.astype(BF) for v in x]
            gram = [mm_nt(v, v) for v in xb]
            half = [v.astype(BF) for v in gram]
            square = [mm(v, v) for v in half]
            poly = [(coef_second * a + coef_third * b).astype(BF) for a, b in zip(gram, square)]
            for k in range(KINDS):
                y = coef_first * x[k] + mm(poly[k], xb[k])
                if i is None:
                    xs[k] = y
                else:
                    wn[k] = (wf[k, mine(i)] - y).astype(BF)


        def second(i):
            x = qn[:, :, cut(mine(i))].reshape(2 * rows, size)
            ox[i] = fast_apply(x, wn[1], wn[2], wn[0]).reshape(2 * nh, share, size)
            for p in order:
                for c in range(2):
                    if p > 0:
                        deal_next(i, c, p).start()
                    else:

                        @pl.when(lane != c)
                        def _():
                            deal_next(i, c, p).start()

            keep_next(i).start()

        def ready_theirs(i):
            @pl.when(theirs(i) < heads)
            def _():
                gradients_theirs(i)

        def add_mine(i):
            @pl.when(mine(i) < heads)
            def _():
                add_theirs(i)

        def ready_mine(i):
            @pl.when((i < slots) & (mine(i) < heads))
            def _():
                gradients_mine(i)
                add_theirs(i)

        def first_of(h):
            @pl.when(h < heads)
            def _():
                first(h)

        first_loads = opening()
        for copy in first_loads:
            copy.start()

        @pl.when(z > 0)
        def _():
            pl.semaphore_signal(barrier, inc=1, device_id=(hd, tok - 2), device_id_type=MESH)

        @pl.when(z < nz - 1)
        def _():
            pl.semaphore_signal(barrier, inc=1, device_id=(hd, tok + 2), device_id_type=MESH)

        greet_plane()
        load_head(1, cut(mine(0)), pl.ds(mine(0), 1))
        rest = heads - 2

        def early_waits():
            first_loads[0].wait()
            two = wf.at[pl.ds(1, 2), theirs(0)]
            pltpu.make_async_copy(two, two, ld.at[3, 1]).wait()

        def late_waits():
            for copy in first_loads[3:]:
                copy.wait()
            if rest > 0:
                load_head(2, pl.ds(2 * size, rest * size), pl.ds(2, rest))
            load_first.start()
            load_next.start()


        def enter(k):
            if k == 0:
                pl.semaphore_wait(barrier, 1 + 2 * (nh - 1) + inner)

        gradients_theirs(0, enter, (early_waits, late_waits))
        wait_head(1, 1)
        gradients_mine(0)
        add_theirs(0)
        if heads > 2:
            wait_head(2, rest)

            @pl.loop(1, slots)
            def _(i):
                ready_theirs(i)

        push_next.start()
        if slots > 1:

            @pl.when(mine(1) < heads)
            def _():
                gradients_mine(1)

        hops = max(nz - 3, 0)
        late = LAG * hops if turn_at - LAG * hops >= per * (slots - 2) else LAG_ALONE * hops
        behind, offset = late // per, late % per
        defer = middle & (mine(slots - 1) < heads)

        load_both.wait()

        @pl.loop(0, slots + behind)
        def _(r):
            base = per * r
            i = r - 1 - behind

            def done(work):
                def run():
                    @pl.when((i >= 0) & jnp.logical_not(defer & (i == slots - 2)))
                    def _():
                        work()

                return run

            def begin():
                @pl.when(i == 0)
                def _():
                    push_next.wait_recv()

                gather(i)

            start = offset
            stride = max(PIECES // 4, 1)
            work = {stride: [lambda: ready_mine(r + 2)]}
            firsts = (heads + 1) // 2
            for n in range(firsts):
                work[stride * (2 * n + 3)] = [lambda n=n: first_of(firsts * r + n)]
            tail = []
            for n, item in enumerate([begin, None, sweep, sweep, None, lambda: sweep(i), lambda: second(i)]):
                if item is None:
                    continue
                if start + stride * n < per:
                    work.setdefault(start + stride * n, []).append(done(item))
                else:
                    tail.append(done(item))
            for t in range(per):
                pass_on(base + t)
                if t == 0 and slots > 1:

                    @pl.when(r == 0)
                    def _():
                        add_mine(1)

                for item in work.get(t, []):
                    item()
            for item in tail:
                item()

        @pl.loop(per * (slots + behind), per * slots + LAG_ALONE * hops)
        def _(t):
            pass_on(t)

        @pl.loop(jnp.where(defer, max(slots - 2, 0), slots - 1), slots)
        def _(i):
            @pl.when(mine(i) < heads)
            def _():
                if slots <= 2:

                    @pl.when(i == 0)
                    def _():
                            push_next.wait_recv()

                gather(i)
                for s in range(NS_STEPS):
                    sweep(i if s == NS_STEPS - 1 else None)
                second(i)

        push_next.wait_send()

        @pl.loop(0, slots)
        def _(i):
            @pl.when(theirs(i) < heads)
            def _():
                pltpu.make_async_copy(sent.at[i], sent.at[i], sw_s.at[i]).wait()

            @pl.when(mine(i) < heads)
            def _():
                slot = own.at[pl.ds(KINDS * i, KINDS)]

                @pl.when(z < nz - 1)
                def _():
                    pltpu.make_async_copy(slot, slot, p_s.at[i]).wait()

                @pl.when(z > 0)
                def _():
                    pltpu.make_async_copy(slot, slot, s_s.at[i]).wait()

        @pl.loop(0, slots)
        def _(i):
            part = ox.at[i, 0]

            @pl.when(theirs(i) < heads)
            def _():
                pltpu.make_async_copy(part, part, b_p.at[i]).wait()

            @pl.when(mine(i) < heads)
            def _():
                most = ox.at[i, pl.ds(0, 2 * nh - 1)]
                pltpu.make_async_copy(most, most, b_s.at[i]).wait()
                pltpu.make_async_copy(part, part, b_l.at[i]).wait()

        part = ob.at[:, pl.ds(0, (nh - 1) * share)]
        pltpu.make_async_copy(part, part, a_s.at[0]).wait()
        part = ob.at[:, pl.ds(0, share)]
        pltpu.make_async_copy(part, part, a_s.at[1]).wait()
        for p in range(1, nh):
            part = out.at[0, :, pl.ds(0, heads * size)]
            pltpu.make_async_copy(part, part, a_r.at[p - 1]).wait()
            part = out.at[1, :, pl.ds(0, heads * size)]
            pltpu.make_async_copy(part, part, b_r.at[p - 1]).wait()

    dma = pltpu.SemaphoreType.DMA
    pieces = KINDS * slots * PIECES
    pl.run_scoped(
        main,
        dma((5, 2)), dma((2,)),
        dma((slots,)), dma((PIECES,)), dma((slots,)),
        dma((slots,)), dma((pieces // PAIR,)),
        dma((slots,)), dma((pieces,)),
        dma((2,)), dma((nh - 1,)),
        dma((slots,)), dma((nh - 1,)), dma((slots,)), dma((slots,)),
    )


def solution(mesh):
    nh = mesh.shape["head"]
    nz = mesh.shape["tok"] // 2

    def local(queries, key_rows, value_rows, step_rates, gate_fast, up_fast, down_fast):
        heads, size, _ = gate_fast.shape
        rows = key_rows.shape[0]
        slots = (heads + 1) // 2
        matrices = KINDS * slots
        out_shape = (2, rows // nh, nh * heads * size)
        out_bytes = 2 * out_shape[0] * out_shape[1] * out_shape[2]
        anywhere = pl.BlockSpec(memory_space=pl.ANY)
        stack = pltpu.VMEM((matrices, size, size), BF)
        return pl.pallas_call(
            functools.partial(kernel, nh, nz),
            out_shape=pltpu.VMEM(out_shape, BF),
            in_specs=[anywhere] * 7,
            out_specs=pl.BlockSpec(memory_space=pltpu.VMEM),
            scratch_shapes=[
                pltpu.VMEM((rows, heads * size), BF),
                pltpu.VMEM((2, rows, heads * size), BF),
                pltpu.VMEM((rows, heads * size), BF),
                pltpu.VMEM((rows, heads * size), BF),
                pltpu.VMEM((heads, rows), F32),
                pltpu.VMEM((KINDS, heads, size, size), F32),
                pltpu.VMEM((KINDS, heads, size, size), BF),
                stack,
                pltpu.VMEM((slots, KINDS, size, size), BF),
                pltpu.VMEM((slots, KINDS, size, size), BF),
                stack, stack, stack, stack,
                pltpu.VMEM((KINDS, size, size), F32),
                pltpu.VMEM((KINDS, size, size), F32),
                pltpu.VMEM((KINDS, size, size), BF),
                pltpu.VMEM((heads, rows, size), BF),
                pltpu.VMEM((slots, 2 * nh, rows // nh, size), BF),
            ],
            compiler_params=pltpu.CompilerParams(
                collective_id=0,
                has_side_effects=True,
                vmem_limit_bytes=VMEM_BYTES - out_bytes - 16384,
            ),
        )(queries, key_rows, value_rows, step_rates, gate_fast, up_fast, down_fast)

    placed = (
        P(None, "tok", "head"),
        P("tok", "head"),
        P("tok", "head"),
        P("head", "tok"),
        P("head", None, None),
        P("head", None, None),
        P("head", None, None),
    )
    return jax.shard_map(
        local, mesh=mesh, in_specs=placed, out_specs=P(None, ("tok", "head"), None), check_vma=False
    )
```

```python
import functools

import jax
import jax.numpy as jnp
from jax import lax
from jax.experimental import pallas as pl
from jax.experimental.pallas import tpu as pltpu
from jax.sharding import PartitionSpec as P

NS_STEPS = 3
KINDS = 3
PIECES = 8
PAIR = 2
LAG = 10
LAG_ALONE = 18
VMEM_BYTES = 67043328

coef_first = 3.4445
coef_second = -4.775
coef_third = 2.0315

MESH = pl.DeviceIdType.MESH
BF = jnp.bfloat16
F32 = jnp.float32


def mm(a, b):
    return jnp.dot(a, b, preferred_element_type=F32)


def mm_tn(a, b):
    return lax.dot_general(a, b, (((0,), (0,)), ((), ())), preferred_element_type=F32)


def mm_nt(a, b):
    return lax.dot_general(a, b, (((1,), (1,)), ((), ())), preferred_element_type=F32)


def fast_apply(x, gate, up, down):
    pre = mm(x, gate)
    hidden = (pre / (1.0 + jnp.exp(-pre)) * mm(x, up)).astype(BF)
    return mm(hidden, down).astype(BF)


def kernel(
    nh, nz, q_in, k_in, v_in, r_in, g_in, u_in, d_in, out,
    qb, qn, kb, vb, rb, wf, wh, own, sent, got, pi, si, po, so, mg, xs, wn, ob, ox,
):
    heads, share, size = ob.shape[0], ob.shape[1] // nh, ob.shape[2]
    rows = nh * share
    slots = sent.shape[0]
    piece = size // PIECES
    per = KINDS * PIECES
    hd = lax.axis_index("head")
    tok = lax.axis_index("tok")
    lane = lax.rem(tok, 2)
    z = tok // 2
    partner = (hd, z * 2 + 1 - lane)
    total = per * ((heads + 1 - lane) // 2)
    first_end = z == 0
    last_end = z == nz - 1
    middle = jnp.logical_not(first_end) & jnp.logical_not(last_end)

    def cut(h):
        return pl.ds(h * size if isinstance(h, int) else pl.multiple_of(h * size, size), size)

    def mine(i):
        return 2 * i + lane

    def theirs(i):
        return 2 * i + 1 - lane

    def main(ld, qs, sw_s, sw_p, sw_r, p_s, p_r, s_s, s_r, a_s, a_r, b_s, b_r, b_p, b_l):
        barrier = pltpu.get_barrier_semaphore()

        inner = (z > 0).astype(jnp.int32) + (z < nz - 1).astype(jnp.int32)

        def greet_plane():
            pl.semaphore_signal(barrier, inc=1, device_id=partner, device_id_type=MESH)
            for p in range(1, nh):
                for c in range(2):
                    pl.semaphore_signal(
                        barrier, inc=1, device_id=(lax.rem(hd + p, nh), 2 * z + c), device_id_type=MESH
                    )

        def load_head(stage, columns, some):
            pltpu.make_async_copy(k_in.at[:, columns], kb.at[:, columns], ld.at[stage, 0]).start()
            for k, src in ((1, g_in), (2, u_in)):
                pltpu.make_async_copy(src.at[some], wf.at[k, some], ld.at[stage, 1]).start()
            pltpu.make_async_copy(v_in.at[:, columns], vb.at[:, columns], ld.at[stage, 0]).start()
            pltpu.make_async_copy(d_in.at[some], wf.at[0, some], ld.at[stage, 1]).start()

        def wait_head(stage, count):
            both = q_in.at[:, :, pl.ds(0, count * size)]
            pltpu.make_async_copy(both, both, ld.at[stage, 0]).wait()
            three = wf.at[:, pl.ds(0, count)]
            pltpu.make_async_copy(three, three, ld.at[stage, 1]).wait()

        def opening():
            h = theirs(0)
            some = pl.ds(h, 1)
            keys = pltpu.make_async_copy(k_in.at[:, cut(h)], kb.at[:, cut(h)], ld.at[0, 0])
            values = pltpu.make_async_copy(v_in.at[:, cut(h)], vb.at[:, cut(h)], ld.at[0, 1])
            gates = pltpu.make_async_copy(g_in.at[some], wf.at[1, some], ld.at[3, 1])
            ups = pltpu.make_async_copy(u_in.at[some], wf.at[2, some], ld.at[3, 1])
            downs = pltpu.make_async_copy(d_in.at[some], wf.at[0, some], ld.at[4, 1])
            return keys, gates, ups, values, downs, load_rates

        load_rates = pltpu.make_async_copy(r_in, rb, ld.at[3, 0])
        load_first = pltpu.make_async_copy(q_in.at[0], qb, ld.at[4, 0])
        load_next = pltpu.make_async_copy(q_in.at[1], qn.at[lane], ld.at[4, 0])
        load_both = pltpu.make_async_copy(q_in, q_in, ld.at[4, 0])
        push_next = pltpu.make_async_remote_copy(
            q_in.at[1], qn.at[lane], qs.at[0], qs.at[1], device_id=partner, device_id_type=MESH
        )

        def place(t):
            return t // PIECES, pl.ds(pl.multiple_of(lax.rem(t, PIECES) * piece, piece), piece)

        def place_right(t):
            span = PAIR * piece
            each = PIECES // PAIR
            return t // each, pl.ds(pl.multiple_of(lax.rem(t, each) * span, span), span)

        def right(src, t):
            m, part = place_right(t)
            return pltpu.make_async_remote_copy(
                src.at[m, part], pi.at[m, part], p_s.at[t // (per // PAIR)], p_r.at[t],
                device_id=(hd, tok + 2), device_id_type=MESH,
            )

        def left(src, t):
            m, part = place(t)
            return pltpu.make_async_remote_copy(
                src.at[m, part], si.at[m, part], s_s.at[t // per], s_r.at[t],
                device_id=(hd, tok - 2), device_id_type=MESH,
            )

        def swap(i, k):
            return pltpu.make_async_remote_copy(
                sent.at[i, k], got.at[i, k], sw_s.at[i], sw_r.at[i],
                device_id=partner, device_id_type=MESH,
            )

        def swap_piece(g):
            part = pl.ds(g * piece, piece)
            return pltpu.make_async_remote_copy(
                sent.at[0, 0, part], got.at[0, 0, part], sw_s.at[0], sw_p.at[g],
                device_id=partner, device_id_type=MESH,
            )

        def wide(h):
            return pl.ds(pl.multiple_of((hd * heads + h) * size, size), size)

        def band(peer):
            return pl.ds(pl.multiple_of(peer * share, share), share)

        order = (3, 1, 2, 0) if nh == 4 else tuple(range(nh - 1, -1, -1))

        def other(p):
            if nh != 4 or p == 0:
                return lax.rem(hd + p, nh)
            return (hd + 1 - 2 * lax.rem(hd, 2), lax.rem(hd + 2, 4), 3 - hd)[p - 1]

        def deal(h, p):
            peer = other(p)
            return pltpu.make_async_remote_copy(
                ob.at[h, band(peer)], out.at[0, :, wide(h)], a_s.at[0], a_r.at[p - 1],
                device_id=(peer, tok), device_id_type=MESH,
            )

        def keep(h):
            return pltpu.make_async_copy(ob.at[h, band(hd)], out.at[0, :, wide(h)], a_s.at[1])

        def deal_next(i, c, p):
            peer = other(p)
            return pltpu.make_async_remote_copy(
                ox.at[i, c * nh + peer], out.at[1, :, wide(mine(i))],
                b_s.at[i], b_p.at[i] if p == 0 else b_r.at[p - 1],
                device_id=(peer, 2 * z + c), device_id_type=MESH,
            )

        def keep_next(i):
            return pltpu.make_async_copy(
                ox.at[i, lane * nh + hd], out.at[1, :, wide(mine(i))], b_l.at[i]
            )

        def gradients(h, put, await_early=None, await_late=None):
            if await_early is not None:
                await_early()
            keys = kb[:, cut(h)]
            gate = wf[1, h].astype(BF)
            up = wf[2, h].astype(BF)
            wh[1, h] = gate
            wh[2, h] = up
            zg = mm(keys, gate)
            zu = mm(keys, up)
            sig = 1.0 / (1.0 + jnp.exp(-zg))
            silu = zg * sig
            hidden = (silu * zu).astype(BF)
            if await_late is not None:
                await_late()
            down = wf[0, h].astype(BF)
            wh[0, h] = down
            line = jnp.broadcast_to(rb[pl.ds(h, 1), :], (128, rows))
            column = jnp.transpose(line)
            column = jnp.concatenate([column] * (size // 128), axis=1)
            dout = (-(column * vb[:, cut(h)].astype(F32))).astype(BF)
            put(0, mm_tn(hidden, dout))
            dh = mm_nt(dout, down)
            dzu = (dh * silu).astype(BF)
            dzg = (dh * zu * sig * (1.0 + zg * (1.0 - sig))).astype(BF)
            put(1, mm_tn(keys, dzg))
            put(2, mm_tn(keys, dzu))

        def gradients_theirs(i, before=lambda k: None, waits=()):
            def put(k, part):
                sent[i, k] = part.astype(BF)
                before(k)
                if isinstance(i, int) and k == 0:
                    for g in range(PIECES):
                        swap_piece(g).start()
                else:
                    swap(i, k).start()

            gradients(theirs(i), put, *waits)

        def gradients_mine(i):
            def put(k, part):
                mg[k] = part

            gradients(mine(i), put)

        def add_first():
            for g in range(PIECES):
                part = pl.ds(g * piece, piece)
                swap_piece(g).wait_recv()
                own[0, part] = (mg[0, part] + got[0, 0, part].astype(F32)).astype(BF)

                @pl.when(last_end)
                def _():
                    left(own, g).start()

                if g % PAIR == PAIR - 1:

                    @pl.when(first_end)
                    def _():
                        right(own, g // PAIR).start()

        def add_theirs(i):
            early = isinstance(i, int) and i == 0
            if early:
                add_first()
            begin = 1 if early else 0
            rest_of = got.at[i, pl.ds(begin, KINDS - begin)]
            pltpu.make_async_copy(rest_of, rest_of, sw_r.at[i]).wait()
            for k in range(begin, KINDS):
                own[KINDS * i + k] = (mg[k] + got[i, k].astype(F32)).astype(BF)

                @pl.when(first_end)
                def _():
                    for g in range(PIECES // PAIR):
                        right(own, (KINDS * i + k) * (PIECES // PAIR) + g).start()

                @pl.when(last_end)
                def _():
                    for g in range(PIECES):
                        left(own, per * i + k * PIECES + g).start()

        turn_at = per * (slots - 1)
        alone = (mine(slots - 1) < heads) & (theirs(slots - 1) >= heads)

        def turn(t, far):
            fast = (LAG_ALONE - LAG) * far
            held = jnp.where(t < turn_at + fast, -1, t - LAG_ALONE * far)
            return jnp.where(alone & (t >= turn_at), held, t - LAG * far)

        def pass_on(t):
            @pl.when(middle)
            def _():
                p = turn(t, z - 1)
                s = turn(t, nz - 2 - z)

                @pl.when((p >= 0) & (p < total) & (lax.rem(p, PAIR) == PAIR - 1))
                def _():
                    n = p // PAIR
                    m, part = place_right(n)
                    right(po, n).wait_recv()
                    po[m, part] = (pi[m, part].astype(F32) + own[m, part].astype(F32)).astype(BF)
                    right(po, n).start()

                @pl.when((s >= 0) & (s < total))
                def _():
                    m, part = place(s)
                    left(so, s).wait_recv()
                    so[m, part] = (si[m, part].astype(F32) + own[m, part].astype(F32)).astype(BF)
                    left(so, s).start()

        def first(h):
            ob[h] = fast_apply(qb[:, cut(h)], wh[1, h], wh[2, h], wh[0, h])
            for p in order[:-1]:
                deal(h, p).start()
            keep(h).start()

        def gather_some(i, kinds):
            for k in kinds:
                m = KINDS * i + k

                @pl.when(first_end)
                def _():
                    for g in range(PIECES):
                        part = pl.ds(g * piece, piece)
                        left(own, per * i + k * PIECES + g).wait_recv()
                        xs[k, part] = own[m, part].astype(F32) + si[m, part].astype(F32)

                @pl.when(last_end)
                def _():
                    for g in range(PIECES // PAIR):
                        part = pl.ds(g * PAIR * piece, PAIR * piece)
                        right(own, (KINDS * i + k) * (PIECES // PAIR) + g).wait_recv()
                        xs[k, part] = own[m, part].astype(F32) + pi[m, part].astype(F32)

                @pl.when(middle)
                def _():
                    xs[k] = own[m].astype(F32) + pi[m].astype(F32) + si[m].astype(F32)

            grads = [xs[k] for k in kinds]
            scales = [1.0 / (jnp.sqrt(jnp.sum(v * v)) + 1e-07) for v in grads]
            for k, v, scale in zip(kinds, grads, scales):
                xs[k] = v * scale

        def gather(i):
            gather_some(i, range(KINDS - 1))
            gather_some(i, [KINDS - 1])

        def sweep(i=None):
            x = [xs[k] for k in range(KINDS)]
            xb = [v.astype(BF) for v in x]
            gram = [mm_nt(v, v) for v in xb]
            half = [v.astype(BF) for v in gram]
            square = [mm(v, v) for v in half]
            poly = [(coef_second * a + coef_third * b).astype(BF) for a, b in zip(gram, square)]
            for k in range(KINDS):
                y = coef_first * x[k] + mm(poly[k], xb[k])
                if i is None:
                    xs[k] = y
                else:
                    wn[k] = (wf[k, mine(i)] - y).astype(BF)


        def second(i):
            x = qn[:, :, cut(mine(i))].reshape(2 * rows, size)
            ox[i] = fast_apply(x, wn[1], wn[2], wn[0]).reshape(2 * nh, share, size)
            for p in order:
                for c in range(2):
                    if p > 0:
                        deal_next(i, c, p).start()
                    else:

                        @pl.when(lane != c)
                        def _():
                            deal_next(i, c, p).start()

            keep_next(i).start()

        def ready_theirs(i):
            @pl.when(theirs(i) < heads)
            def _():
                gradients_theirs(i)

        def add_mine(i):
            @pl.when(mine(i) < heads)
            def _():
                add_theirs(i)

        def ready_mine(i):
            @pl.when((i < slots) & (mine(i) < heads))
            def _():
                gradients_mine(i)
                add_theirs(i)

        def first_of(h):
            @pl.when(h < heads)
            def _():
                first(h)

        first_loads = opening()
        for copy in first_loads:
            copy.start()

        @pl.when(z > 0)
        def _():
            pl.semaphore_signal(barrier, inc=1, device_id=(hd, tok - 2), device_id_type=MESH)

        @pl.when(z < nz - 1)
        def _():
            pl.semaphore_signal(barrier, inc=1, device_id=(hd, tok + 2), device_id_type=MESH)

        greet_plane()
        load_head(1, cut(mine(0)), pl.ds(mine(0), 1))
        rest = heads - 2

        def early_waits():
            first_loads[0].wait()
            two = wf.at[pl.ds(1, 2), theirs(0)]
            pltpu.make_async_copy(two, two, ld.at[3, 1]).wait()

        def late_waits():
            for copy in first_loads[3:]:
                copy.wait()
            if rest > 0:
                load_head(2, pl.ds(2 * size, rest * size), pl.ds(2, rest))
            load_first.start()
            load_next.start()


        def enter(k):
            if k == 0:
                pl.semaphore_wait(barrier, 1 + 2 * (nh - 1) + inner)

        gradients_theirs(0, enter, (early_waits, late_waits))
        wait_head(1, 1)
        gradients_mine(0)
        add_theirs(0)
        if heads > 2:
            wait_head(2, rest)

            @pl.loop(1, slots)
            def _(i):
                ready_theirs(i)

        push_next.start()
        if slots > 1:

            @pl.when(mine(1) < heads)
            def _():
                gradients_mine(1)

        hops = max(nz - 3, 0)
        late = LAG * hops if turn_at - LAG * hops >= per * (slots - 2) else LAG_ALONE * hops
        behind, offset = late // per, late % per
        defer = middle & (mine(slots - 1) < heads)

        load_both.wait()

        @pl.loop(0, slots + behind)
        def _(r):
            base = per * r
            i = r - 1 - behind

            def done(work):
                def run():
                    @pl.when((i >= 0) & jnp.logical_not(defer & (i == slots - 2)))
                    def _():
                        work()

                return run

            def begin():
                @pl.when(i == 0)
                def _():
                    push_next.wait_recv()

                gather(i)

            start = offset
            stride = max(PIECES // 4, 1)
            work = {stride: [lambda: ready_mine(r + 2)]}
            firsts = (heads + 1) // 2
            for n in range(firsts):
                work[stride * (2 * n + 3)] = [lambda n=n: first_of(firsts * r + n)]
            tail = []
            for n, item in enumerate([begin, None, sweep, sweep, None, lambda: sweep(i), lambda: second(i)]):
                if item is None:
                    continue
                if start + stride * n < per:
                    work.setdefault(start + stride * n, []).append(done(item))
                else:
                    tail.append(done(item))
            for t in range(per):
                pass_on(base + t)
                if t == 0 and slots > 1:

                    @pl.when(r == 0)
                    def _():
                        add_mine(1)

                for item in work.get(t, []):
                    item()
            for item in tail:
                item()

        @pl.when(middle)
        def _():
            @pl.loop(per * (slots + behind), per * slots + LAG_ALONE * hops)
            def _(t):
                pass_on(t)

        @pl.loop(jnp.where(defer, max(slots - 2, 0), slots - 1), slots)
        def _(i):
            @pl.when(mine(i) < heads)
            def _():
                if slots <= 2:

                    @pl.when(i == 0)
                    def _():
                            push_next.wait_recv()

                gather(i)
                for s in range(NS_STEPS):
                    sweep(i if s == NS_STEPS - 1 else None)
                second(i)

        push_next.wait_send()

        @pl.loop(0, slots)
        def _(i):
            @pl.when(theirs(i) < heads)
            def _():
                pltpu.make_async_copy(sent.at[i], sent.at[i], sw_s.at[i]).wait()

            @pl.when(mine(i) < heads)
            def _():
                slot = own.at[pl.ds(KINDS * i, KINDS)]

                @pl.when(z < nz - 1)
                def _():
                    pltpu.make_async_copy(slot, slot, p_s.at[i]).wait()

                @pl.when(z > 0)
                def _():
                    pltpu.make_async_copy(slot, slot, s_s.at[i]).wait()

        @pl.loop(0, slots)
        def _(i):
            part = ox.at[i, 0]

            @pl.when(theirs(i) < heads)
            def _():
                pltpu.make_async_copy(part, part, b_p.at[i]).wait()

            @pl.when(mine(i) < heads)
            def _():
                most = ox.at[i, pl.ds(0, 2 * nh - 1)]
                pltpu.make_async_copy(most, most, b_s.at[i]).wait()
                pltpu.make_async_copy(part, part, b_l.at[i]).wait()

        part = ob.at[:, pl.ds(0, (nh - 1) * share)]
        pltpu.make_async_copy(part, part, a_s.at[0]).wait()
        part = ob.at[:, pl.ds(0, share)]
        pltpu.make_async_copy(part, part, a_s.at[1]).wait()
        for p in range(1, nh):
            part = out.at[0, :, pl.ds(0, heads * size)]
            pltpu.make_async_copy(part, part, a_r.at[p - 1]).wait()
            part = out.at[1, :, pl.ds(0, heads * size)]
            pltpu.make_async_copy(part, part, b_r.at[p - 1]).wait()

    dma = pltpu.SemaphoreType.DMA
    pieces = KINDS * slots * PIECES
    pl.run_scoped(
        main,
        dma((5, 2)), dma((2,)),
        dma((slots,)), dma((PIECES,)), dma((slots,)),
        dma((slots,)), dma((pieces // PAIR,)),
        dma((slots,)), dma((pieces,)),
        dma((2,)), dma((nh - 1,)),
        dma((slots,)), dma((nh - 1,)), dma((slots,)), dma((slots,)),
    )


def solution(mesh):
    nh = mesh.shape["head"]
    nz = mesh.shape["tok"] // 2

    def local(queries, key_rows, value_rows, step_rates, gate_fast, up_fast, down_fast):
        heads, size, _ = gate_fast.shape
        rows = key_rows.shape[0]
        slots = (heads + 1) // 2
        matrices = KINDS * slots
        out_shape = (2, rows // nh, nh * heads * size)
        out_bytes = 2 * out_shape[0] * out_shape[1] * out_shape[2]
        anywhere = pl.BlockSpec(memory_space=pl.ANY)
        stack = pltpu.VMEM((matrices, size, size), BF)
        return pl.pallas_call(
            functools.partial(kernel, nh, nz),
            out_shape=pltpu.VMEM(out_shape, BF),
            in_specs=[anywhere] * 7,
            out_specs=pl.BlockSpec(memory_space=pltpu.VMEM),
            scratch_shapes=[
                pltpu.VMEM((rows, heads * size), BF),
                pltpu.VMEM((2, rows, heads * size), BF),
                pltpu.VMEM((rows, heads * size), BF),
                pltpu.VMEM((rows, heads * size), BF),
                pltpu.VMEM((heads, rows), F32),
                pltpu.VMEM((KINDS, heads, size, size), F32),
                pltpu.VMEM((KINDS, heads, size, size), BF),
                stack,
                pltpu.VMEM((slots, KINDS, size, size), BF),
                pltpu.VMEM((slots, KINDS, size, size), BF),
                stack, stack, stack, stack,
                pltpu.VMEM((KINDS, size, size), F32),
                pltpu.VMEM((KINDS, size, size), F32),
                pltpu.VMEM((KINDS, size, size), BF),
                pltpu.VMEM((heads, rows, size), BF),
                pltpu.VMEM((slots, 2 * nh, rows // nh, size), BF),
            ],
            compiler_params=pltpu.CompilerParams(
                collective_id=0,
                has_side_effects=True,
                vmem_limit_bytes=VMEM_BYTES - out_bytes - 16384,
            ),
        )(queries, key_rows, value_rows, step_rates, gate_fast, up_fast, down_fast)

    placed = (
        P(None, "tok", "head"),
        P("tok", "head"),
        P("tok", "head"),
        P("head", "tok"),
        P("head", None, None),
        P("head", None, None),
        P("head", None, None),
    )
    return jax.shard_map(
        local, mesh=mesh, in_specs=placed, out_specs=P(None, ("tok", "head"), None), check_vma=False
    )
```

```python
import functools

import jax
import jax.numpy as jnp
from jax import lax
from jax.experimental import pallas as pl
from jax.experimental.pallas import tpu as pltpu
from jax.sharding import PartitionSpec as P

NS_STEPS = 3
KINDS = 3
PIECES = 8
PAIR = 2
LAG = 10
LAG_ALONE = 16
VMEM_BYTES = 67043328

coef_first = 3.4445
coef_second = -4.775
coef_third = 2.0315

MESH = pl.DeviceIdType.MESH
BF = jnp.bfloat16
F32 = jnp.float32


def mm(a, b):
    return jnp.dot(a, b, preferred_element_type=F32)


def mm_tn(a, b):
    return lax.dot_general(a, b, (((0,), (0,)), ((), ())), preferred_element_type=F32)


def mm_nt(a, b):
    return lax.dot_general(a, b, (((1,), (1,)), ((), ())), preferred_element_type=F32)


def fast_apply(x, gate, up, down):
    pre = mm(x, gate)
    hidden = (pre / (1.0 + jnp.exp(-pre)) * mm(x, up)).astype(BF)
    return mm(hidden, down).astype(BF)


def kernel(
    nh, nz, q_in, k_in, v_in, r_in, g_in, u_in, d_in, out,
    qb, qn, kb, vb, rb, wf, wh, own, sent, got, pi, si, po, so, mg, xs, wn, ob, ox,
):
    heads, share, size = ob.shape[0], ob.shape[1] // nh, ob.shape[2]
    rows = nh * share
    slots = sent.shape[0]
    piece = size // PIECES
    per = KINDS * PIECES
    hd = lax.axis_index("head")
    tok = lax.axis_index("tok")
    lane = lax.rem(tok, 2)
    z = tok // 2
    partner = (hd, z * 2 + 1 - lane)
    total = per * ((heads + 1 - lane) // 2)
    first_end = z == 0
    last_end = z == nz - 1
    middle = jnp.logical_not(first_end) & jnp.logical_not(last_end)

    def cut(h):
        return pl.ds(h * size if isinstance(h, int) else pl.multiple_of(h * size, size), size)

    def mine(i):
        return 2 * i + lane

    def theirs(i):
        return 2 * i + 1 - lane

    def main(ld, qs, sw_s, sw_p, sw_r, p_s, p_r, s_s, s_r, a_s, a_r, b_s, b_r, b_p, b_l):
        barrier = pltpu.get_barrier_semaphore()

        inner = (z > 0).astype(jnp.int32) + (z < nz - 1).astype(jnp.int32)

        def greet_plane():
            pl.semaphore_signal(barrier, inc=1, device_id=partner, device_id_type=MESH)
            for p in range(1, nh):
                for c in range(2):
                    pl.semaphore_signal(
                        barrier, inc=1, device_id=(lax.rem(hd + p, nh), 2 * z + c), device_id_type=MESH
                    )

        def load_head(stage, columns, some):
            pltpu.make_async_copy(k_in.at[:, columns], kb.at[:, columns], ld.at[stage, 0]).start()
            for k, src in ((1, g_in), (2, u_in)):
                pltpu.make_async_copy(src.at[some], wf.at[k, some], ld.at[stage, 1]).start()
            pltpu.make_async_copy(v_in.at[:, columns], vb.at[:, columns], ld.at[stage, 0]).start()
            pltpu.make_async_copy(d_in.at[some], wf.at[0, some], ld.at[stage, 1]).start()

        def wait_head(stage, count):
            both = q_in.at[:, :, pl.ds(0, count * size)]
            pltpu.make_async_copy(both, both, ld.at[stage, 0]).wait()
            three = wf.at[:, pl.ds(0, count)]
            pltpu.make_async_copy(three, three, ld.at[stage, 1]).wait()

        def opening():
            h = theirs(0)
            some = pl.ds(h, 1)
            keys = pltpu.make_async_copy(k_in.at[:, cut(h)], kb.at[:, cut(h)], ld.at[0, 0])
            values = pltpu.make_async_copy(v_in.at[:, cut(h)], vb.at[:, cut(h)], ld.at[0, 1])
            gates = pltpu.make_async_copy(g_in.at[some], wf.at[1, some], ld.at[3, 1])
            ups = pltpu.make_async_copy(u_in.at[some], wf.at[2, some], ld.at[3, 1])
            downs = pltpu.make_async_copy(d_in.at[some], wf.at[0, some], ld.at[4, 1])
            return keys, gates, ups, values, downs, load_rates

        load_rates = pltpu.make_async_copy(r_in, rb, ld.at[3, 0])
        load_first = pltpu.make_async_copy(q_in.at[0], qb, ld.at[4, 0])
        load_next = pltpu.make_async_copy(q_in.at[1], qn.at[lane], ld.at[4, 0])
        load_both = pltpu.make_async_copy(q_in, q_in, ld.at[4, 0])
        push_next = pltpu.make_async_remote_copy(
            q_in.at[1], qn.at[lane], qs.at[0], qs.at[1], device_id=partner, device_id_type=MESH
        )

        def place(t):
            return t // PIECES, pl.ds(pl.multiple_of(lax.rem(t, PIECES) * piece, piece), piece)

        def place_right(t):
            span = PAIR * piece
            each = PIECES // PAIR
            return t // each, pl.ds(pl.multiple_of(lax.rem(t, each) * span, span), span)

        def right(src, t):
            m, part = place_right(t)
            return pltpu.make_async_remote_copy(
                src.at[m, part], pi.at[m, part], p_s.at[t // (per // PAIR)], p_r.at[t],
                device_id=(hd, tok + 2), device_id_type=MESH,
            )

        def left(src, t):
            m, part = place(t)
            return pltpu.make_async_remote_copy(
                src.at[m, part], si.at[m, part], s_s.at[t // per], s_r.at[t],
                device_id=(hd, tok - 2), device_id_type=MESH,
            )

        def swap(i, k):
            return pltpu.make_async_remote_copy(
                sent.at[i, k], got.at[i, k], sw_s.at[i], sw_r.at[i],
                device_id=partner, device_id_type=MESH,
            )

        def swap_piece(g):
            part = pl.ds(g * piece, piece)
            return pltpu.make_async_remote_copy(
                sent.at[0, 0, part], got.at[0, 0, part], sw_s.at[0], sw_p.at[g],
                device_id=partner, device_id_type=MESH,
            )

        def wide(h):
            return pl.ds(pl.multiple_of((hd * heads + h) * size, size), size)

        def band(peer):
            return pl.ds(pl.multiple_of(peer * share, share), share)

        order = (3, 1, 2, 0) if nh == 4 else tuple(range(nh - 1, -1, -1))

        def other(p):
            if nh != 4 or p == 0:
                return lax.rem(hd + p, nh)
            return (hd + 1 - 2 * lax.rem(hd, 2), lax.rem(hd + 2, 4), 3 - hd)[p - 1]

        def deal(h, p):
            peer = other(p)
            return pltpu.make_async_remote_copy(
                ob.at[h, band(peer)], out.at[0, :, wide(h)], a_s.at[0], a_r.at[p - 1],
                device_id=(peer, tok), device_id_type=MESH,
            )

        def keep(h):
            return pltpu.make_async_copy(ob.at[h, band(hd)], out.at[0, :, wide(h)], a_s.at[1])

        def deal_next(i, c, p):
            peer = other(p)
            return pltpu.make_async_remote_copy(
                ox.at[i, c * nh + peer], out.at[1, :, wide(mine(i))],
                b_s.at[i], b_p.at[i] if p == 0 else b_r.at[p - 1],
                device_id=(peer, 2 * z + c), device_id_type=MESH,
            )

        def keep_next(i):
            return pltpu.make_async_copy(
                ox.at[i, lane * nh + hd], out.at[1, :, wide(mine(i))], b_l.at[i]
            )

        def gradients(h, put, await_early=None, await_late=None):
            if await_early is not None:
                await_early()
            keys = kb[:, cut(h)]
            gate = wf[1, h].astype(BF)
            up = wf[2, h].astype(BF)
            wh[1, h] = gate
            wh[2, h] = up
            zg = mm(keys, gate)
            zu = mm(keys, up)
            sig = 1.0 / (1.0 + jnp.exp(-zg))
            silu = zg * sig
            hidden = (silu * zu).astype(BF)
            if await_late is not None:
                await_late()
            down = wf[0, h].astype(BF)
            wh[0, h] = down
            line = jnp.broadcast_to(rb[pl.ds(h, 1), :], (128, rows))
            column = jnp.transpose(line)
            column = jnp.concatenate([column] * (size // 128), axis=1)
            dout = (-(column * vb[:, cut(h)].astype(F32))).astype(BF)
            put(0, mm_tn(hidden, dout))
            dh = mm_nt(dout, down)
            dzu = (dh * silu).astype(BF)
            dzg = (dh * zu * sig * (1.0 + zg * (1.0 - sig))).astype(BF)
            put(1, mm_tn(keys, dzg))
            put(2, mm_tn(keys, dzu))

        def gradients_theirs(i, before=lambda k: None, waits=()):
            def put(k, part):
                sent[i, k] = part.astype(BF)
                before(k)
                if isinstance(i, int) and k == 0:
                    for g in range(PIECES):
                        swap_piece(g).start()
                else:
                    swap(i, k).start()

            gradients(theirs(i), put, *waits)

        def gradients_mine(i):
            def put(k, part):
                mg[k] = part

            gradients(mine(i), put)

        def add_first():
            for g in range(PIECES):
                part = pl.ds(g * piece, piece)
                swap_piece(g).wait_recv()
                own[0, part] = (mg[0, part] + got[0, 0, part].astype(F32)).astype(BF)

                @pl.when(last_end)
                def _():
                    left(own, g).start()

                if g % PAIR == PAIR - 1:

                    @pl.when(first_end)
                    def _():
                        right(own, g // PAIR).start()

        def add_theirs(i):
            early = isinstance(i, int) and i == 0
            if early:
                add_first()
            begin = 1 if early else 0
            rest_of = got.at[i, pl.ds(begin, KINDS - begin)]
            pltpu.make_async_copy(rest_of, rest_of, sw_r.at[i]).wait()
            for k in range(begin, KINDS):
                own[KINDS * i + k] = (mg[k] + got[i, k].astype(F32)).astype(BF)

                @pl.when(first_end)
                def _():
                    for g in range(PIECES // PAIR):
                        right(own, (KINDS * i + k) * (PIECES // PAIR) + g).start()

                @pl.when(last_end)
                def _():
                    for g in range(PIECES):
                        left(own, per * i + k * PIECES + g).start()

        turn_at = per * (slots - 1)
        alone = (mine(slots - 1) < heads) & (theirs(slots - 1) >= heads)

        def turn(t, far):
            fast = (LAG_ALONE - LAG) * far
            held = jnp.where(t < turn_at + fast, -1, t - LAG_ALONE * far)
            return jnp.where(alone & (t >= turn_at), held, t - LAG * far)

        def pass_on(t):
            @pl.when(middle)
            def _():
                p = turn(t, z - 1)
                s = turn(t, nz - 2 - z)

                @pl.when((p >= 0) & (p < total) & (lax.rem(p, PAIR) == PAIR - 1))
                def _():
                    n = p // PAIR
                    m, part = place_right(n)
                    right(po, n).wait_recv()
                    po[m, part] = (pi[m, part].astype(F32) + own[m, part].astype(F32)).astype(BF)
                    right(po, n).start()

                @pl.when((s >= 0) & (s < total))
                def _():
                    m, part = place(s)
                    left(so, s).wait_recv()
                    so[m, part] = (si[m, part].astype(F32) + own[m, part].astype(F32)).astype(BF)
                    left(so, s).start()

        def first(h):
            ob[h] = fast_apply(qb[:, cut(h)], wh[1, h], wh[2, h], wh[0, h])
            for p in order[:-1]:
                deal(h, p).start()
            keep(h).start()

        def gather_some(i, kinds):
            for k in kinds:
                m = KINDS * i + k

                @pl.when(first_end)
                def _():
                    for g in range(PIECES):
                        part = pl.ds(g * piece, piece)
                        left(own, per * i + k * PIECES + g).wait_recv()
                        xs[k, part] = own[m, part].astype(F32) + si[m, part].astype(F32)

                @pl.when(last_end)
                def _():
                    for g in range(PIECES // PAIR):
                        part = pl.ds(g * PAIR * piece, PAIR * piece)
                        right(own, (KINDS * i + k) * (PIECES // PAIR) + g).wait_recv()
                        xs[k, part] = own[m, part].astype(F32) + pi[m, part].astype(F32)

                @pl.when(middle)
                def _():
                    xs[k] = own[m].astype(F32) + pi[m].astype(F32) + si[m].astype(F32)

            grads = [xs[k] for k in kinds]
            scales = [1.0 / (jnp.sqrt(jnp.sum(v * v)) + 1e-07) for v in grads]
            for k, v, scale in zip(kinds, grads, scales):
                xs[k] = v * scale

        def gather(i):
            gather_some(i, range(KINDS - 1))
            gather_some(i, [KINDS - 1])

        def sweep(i=None):
            x = [xs[k] for k in range(KINDS)]
            xb = [v.astype(BF) for v in x]
            gram = [mm_nt(v, v) for v in xb]
            half = [v.astype(BF) for v in gram]
            square = [mm(v, v) for v in half]
            poly = [(coef_second * a + coef_third * b).astype(BF) for a, b in zip(gram, square)]
            for k in range(KINDS):
                y = coef_first * x[k] + mm(poly[k], xb[k])
                if i is None:
                    xs[k] = y
                else:
                    wn[k] = (wf[k, mine(i)] - y).astype(BF)


        def second(i):
            x = qn[:, :, cut(mine(i))].reshape(2 * rows, size)
            ox[i] = fast_apply(x, wn[1], wn[2], wn[0]).reshape(2 * nh, share, size)
            for p in order:
                for c in range(2):
                    if p > 0:
                        deal_next(i, c, p).start()
                    else:

                        @pl.when(lane != c)
                        def _():
                            deal_next(i, c, p).start()

            keep_next(i).start()

        def ready_theirs(i):
            @pl.when(theirs(i) < heads)
            def _():
                gradients_theirs(i)

        def add_mine(i):
            @pl.when(mine(i) < heads)
            def _():
                add_theirs(i)

        def ready_mine(i):
            @pl.when((i < slots) & (mine(i) < heads))
            def _():
                gradients_mine(i)
                add_theirs(i)

        def first_of(h):
            @pl.when(h < heads)
            def _():
                first(h)

        first_loads = opening()
        for copy in first_loads:
            copy.start()

        @pl.when(z > 0)
        def _():
            pl.semaphore_signal(barrier, inc=1, device_id=(hd, tok - 2), device_id_type=MESH)

        @pl.when(z < nz - 1)
        def _():
            pl.semaphore_signal(barrier, inc=1, device_id=(hd, tok + 2), device_id_type=MESH)

        greet_plane()
        load_head(1, cut(mine(0)), pl.ds(mine(0), 1))
        rest = heads - 2

        def early_waits():
            first_loads[0].wait()
            two = wf.at[pl.ds(1, 2), theirs(0)]
            pltpu.make_async_copy(two, two, ld.at[3, 1]).wait()

        def late_waits():
            for copy in first_loads[3:]:
                copy.wait()
            if rest > 0:
                load_head(2, pl.ds(2 * size, rest * size), pl.ds(2, rest))
            load_first.start()
            load_next.start()


        def enter(k):
            if k == 0:
                pl.semaphore_wait(barrier, 1 + 2 * (nh - 1) + inner)

        gradients_theirs(0, enter, (early_waits, late_waits))
        wait_head(1, 1)
        gradients_mine(0)
        add_theirs(0)
        if heads > 2:
            wait_head(2, rest)

            @pl.loop(1, slots)
            def _(i):
                ready_theirs(i)

        push_next.start()
        if slots > 1:

            @pl.when(mine(1) < heads)
            def _():
                gradients_mine(1)

        hops = max(nz - 3, 0)
        late = LAG * hops if turn_at - LAG * hops >= per * (slots - 2) else LAG_ALONE * hops
        behind, offset = late // per, late % per
        defer = middle & (mine(slots - 1) < heads)

        load_both.wait()

        @pl.loop(0, slots + behind)
        def _(r):
            base = per * r
            i = r - 1 - behind

            def done(work):
                def run():
                    @pl.when((i >= 0) & jnp.logical_not(defer & (i == slots - 2)))
                    def _():
                        work()

                return run

            def begin():
                @pl.when(i == 0)
                def _():
                    push_next.wait_recv()

                gather(i)

            start = offset
            stride = max(PIECES // 4, 1)
            work = {stride: [lambda: ready_mine(r + 2)]}
            firsts = (heads + 1) // 2
            for n in range(firsts):
                work[stride * (2 * n + 3)] = [lambda n=n: first_of(firsts * r + n)]
            tail = []
            for n, item in enumerate([begin, None, sweep, sweep, None, lambda: sweep(i), lambda: second(i)]):
                if item is None:
                    continue
                if start + stride * n < per:
                    work.setdefault(start + stride * n, []).append(done(item))
                else:
                    tail.append(done(item))
            for t in range(per):
                pass_on(base + t)
                if t == 0 and slots > 1:

                    @pl.when(r == 0)
                    def _():
                        add_mine(1)

                for item in work.get(t, []):
                    item()
            for item in tail:
                item()

        @pl.when(middle)
        def _():
            @pl.loop(per * (slots + behind), per * slots + LAG_ALONE * hops)
            def _(t):
                pass_on(t)

        @pl.loop(jnp.where(defer, max(slots - 2, 0), slots - 1), slots)
        def _(i):
            @pl.when(mine(i) < heads)
            def _():
                if slots <= 2:

                    @pl.when(i == 0)
                    def _():
                            push_next.wait_recv()

                gather(i)
                for s in range(NS_STEPS):
                    sweep(i if s == NS_STEPS - 1 else None)
                second(i)

        push_next.wait_send()

        @pl.loop(0, slots)
        def _(i):
            @pl.when(theirs(i) < heads)
            def _():
                pltpu.make_async_copy(sent.at[i], sent.at[i], sw_s.at[i]).wait()

            @pl.when(mine(i) < heads)
            def _():
                slot = own.at[pl.ds(KINDS * i, KINDS)]

                @pl.when(z < nz - 1)
                def _():
                    pltpu.make_async_copy(slot, slot, p_s.at[i]).wait()

                @pl.when(z > 0)
                def _():
                    pltpu.make_async_copy(slot, slot, s_s.at[i]).wait()

        @pl.loop(0, slots)
        def _(i):
            part = ox.at[i, 0]

            @pl.when(theirs(i) < heads)
            def _():
                pltpu.make_async_copy(part, part, b_p.at[i]).wait()

            @pl.when(mine(i) < heads)
            def _():
                most = ox.at[i, pl.ds(0, 2 * nh - 1)]
                pltpu.make_async_copy(most, most, b_s.at[i]).wait()
                pltpu.make_async_copy(part, part, b_l.at[i]).wait()

        part = ob.at[:, pl.ds(0, (nh - 1) * share)]
        pltpu.make_async_copy(part, part, a_s.at[0]).wait()
        part = ob.at[:, pl.ds(0, share)]
        pltpu.make_async_copy(part, part, a_s.at[1]).wait()
        for p in range(1, nh):
            part = out.at[0, :, pl.ds(0, heads * size)]
            pltpu.make_async_copy(part, part, a_r.at[p - 1]).wait()
            part = out.at[1, :, pl.ds(0, heads * size)]
            pltpu.make_async_copy(part, part, b_r.at[p - 1]).wait()

    dma = pltpu.SemaphoreType.DMA
    pieces = KINDS * slots * PIECES
    pl.run_scoped(
        main,
        dma((5, 2)), dma((2,)),
        dma((slots,)), dma((PIECES,)), dma((slots,)),
        dma((slots,)), dma((pieces // PAIR,)),
        dma((slots,)), dma((pieces,)),
        dma((2,)), dma((nh - 1,)),
        dma((slots,)), dma((nh - 1,)), dma((slots,)), dma((slots,)),
    )


def solution(mesh):
    nh = mesh.shape["head"]
    nz = mesh.shape["tok"] // 2

    def local(queries, key_rows, value_rows, step_rates, gate_fast, up_fast, down_fast):
        heads, size, _ = gate_fast.shape
        rows = key_rows.shape[0]
        slots = (heads + 1) // 2
        matrices = KINDS * slots
        out_shape = (2, rows // nh, nh * heads * size)
        out_bytes = 2 * out_shape[0] * out_shape[1] * out_shape[2]
        anywhere = pl.BlockSpec(memory_space=pl.ANY)
        stack = pltpu.VMEM((matrices, size, size), BF)
        return pl.pallas_call(
            functools.partial(kernel, nh, nz),
            out_shape=pltpu.VMEM(out_shape, BF),
            in_specs=[anywhere] * 7,
            out_specs=pl.BlockSpec(memory_space=pltpu.VMEM),
            scratch_shapes=[
                pltpu.VMEM((rows, heads * size), BF),
                pltpu.VMEM((2, rows, heads * size), BF),
                pltpu.VMEM((rows, heads * size), BF),
                pltpu.VMEM((rows, heads * size), BF),
                pltpu.VMEM((heads, rows), F32),
                pltpu.VMEM((KINDS, heads, size, size), F32),
                pltpu.VMEM((KINDS, heads, size, size), BF),
                stack,
                pltpu.VMEM((slots, KINDS, size, size), BF),
                pltpu.VMEM((slots, KINDS, size, size), BF),
                stack, stack, stack, stack,
                pltpu.VMEM((KINDS, size, size), F32),
                pltpu.VMEM((KINDS, size, size), F32),
                pltpu.VMEM((KINDS, size, size), BF),
                pltpu.VMEM((heads, rows, size), BF),
                pltpu.VMEM((slots, 2 * nh, rows // nh, size), BF),
            ],
            compiler_params=pltpu.CompilerParams(
                collective_id=0,
                has_side_effects=True,
                vmem_limit_bytes=VMEM_BYTES - out_bytes - 16384,
            ),
        )(queries, key_rows, value_rows, step_rates, gate_fast, up_fast, down_fast)

    placed = (
        P(None, "tok", "head"),
        P("tok", "head"),
        P("tok", "head"),
        P("head", "tok"),
        P("head", None, None),
        P("head", None, None),
        P("head", None, None),
    )
    return jax.shard_map(
        local, mesh=mesh, in_specs=placed, out_specs=P(None, ("tok", "head"), None), check_vma=False
    )
```

```python
import functools

import jax
import jax.numpy as jnp
from jax import lax
from jax.experimental import pallas as pl
from jax.experimental.pallas import tpu as pltpu
from jax.sharding import PartitionSpec as P

NS_STEPS = 3
KINDS = 3
PIECES = 8
PAIR = 2
LAG = 10
LAG_ALONE = 18
VMEM_BYTES = 67043328

coef_first = 3.4445
coef_second = -4.775
coef_third = 2.0315

MESH = pl.DeviceIdType.MESH
BF = jnp.bfloat16
F32 = jnp.float32


def mm(a, b):
    return jnp.dot(a, b, preferred_element_type=F32)


def mm_tn(a, b):
    return lax.dot_general(a, b, (((0,), (0,)), ((), ())), preferred_element_type=F32)


def mm_nt(a, b):
    return lax.dot_general(a, b, (((1,), (1,)), ((), ())), preferred_element_type=F32)


def fast_apply(x, gate, up, down):
    pre = mm(x, gate)
    hidden = (pre / (1.0 + jnp.exp(-pre)) * mm(x, up)).astype(BF)
    return mm(hidden, down).astype(BF)


def kernel(
    nh, nz, q_in, k_in, v_in, r_in, g_in, u_in, d_in, out,
    qb, qn, kb, vb, rb, wf, wh, own, sent, got, pi, si, po, so, mg, xs, wn, ob, ox,
):
    heads, share, size = ob.shape[0], ob.shape[1] // nh, ob.shape[2]
    rows = nh * share
    slots = sent.shape[0]
    piece = size // PIECES
    per = KINDS * PIECES
    hd = lax.axis_index("head")
    tok = lax.axis_index("tok")
    lane = lax.rem(tok, 2)
    z = tok // 2
    partner = (hd, z * 2 + 1 - lane)
    total = per * ((heads + 1 - lane) // 2)
    first_end = z == 0
    last_end = z == nz - 1
    middle = jnp.logical_not(first_end) & jnp.logical_not(last_end)

    def cut(h):
        return pl.ds(h * size if isinstance(h, int) else pl.multiple_of(h * size, size), size)

    def mine(i):
        return 2 * i + lane

    def theirs(i):
        return 2 * i + 1 - lane

    def main(ld, qs, sw_s, sw_p, sw_r, p_s, p_r, s_s, s_r, a_s, a_r, b_s, b_r, b_p, b_l):
        barrier = pltpu.get_barrier_semaphore()

        inner = (z > 0).astype(jnp.int32) + (z < nz - 1).astype(jnp.int32)

        def greet_plane():
            pl.semaphore_signal(barrier, inc=1, device_id=partner, device_id_type=MESH)
            for p in range(1, nh):
                for c in range(2):
                    pl.semaphore_signal(
                        barrier, inc=1, device_id=(lax.rem(hd + p, nh), 2 * z + c), device_id_type=MESH
                    )

        def load_head(stage, columns, some):
            pltpu.make_async_copy(k_in.at[:, columns], kb.at[:, columns], ld.at[stage, 0]).start()
            for k, src in ((1, g_in), (2, u_in)):
                pltpu.make_async_copy(src.at[some], wf.at[k, some], ld.at[stage, 1]).start()
            pltpu.make_async_copy(v_in.at[:, columns], vb.at[:, columns], ld.at[stage, 0]).start()
            pltpu.make_async_copy(d_in.at[some], wf.at[0, some], ld.at[stage, 1]).start()

        def wait_head(stage, count):
            both = q_in.at[:, :, pl.ds(0, count * size)]
            pltpu.make_async_copy(both, both, ld.at[stage, 0]).wait()
            three = wf.at[:, pl.ds(0, count)]
            pltpu.make_async_copy(three, three, ld.at[stage, 1]).wait()

        def opening():
            h = theirs(0)
            some = pl.ds(h, 1)
            keys = pltpu.make_async_copy(k_in.at[:, cut(h)], kb.at[:, cut(h)], ld.at[0, 0])
            values = pltpu.make_async_copy(v_in.at[:, cut(h)], vb.at[:, cut(h)], ld.at[0, 1])
            gates = pltpu.make_async_copy(g_in.at[some], wf.at[1, some], ld.at[3, 1])
            ups = pltpu.make_async_copy(u_in.at[some], wf.at[2, some], ld.at[3, 1])
            downs = pltpu.make_async_copy(d_in.at[some], wf.at[0, some], ld.at[4, 1])
            return keys, gates, ups, values, downs, load_rates

        load_rates = pltpu.make_async_copy(r_in, rb, ld.at[3, 0])
        load_first = pltpu.make_async_copy(q_in.at[0], qb, ld.at[4, 0])
        load_next = pltpu.make_async_copy(q_in.at[1], qn.at[lane], ld.at[4, 0])
        load_both = pltpu.make_async_copy(q_in, q_in, ld.at[4, 0])
        push_next = pltpu.make_async_remote_copy(
            q_in.at[1], qn.at[lane], qs.at[0], qs.at[1], device_id=partner, device_id_type=MESH
        )

        def place(t):
            return t // PIECES, pl.ds(pl.multiple_of(lax.rem(t, PIECES) * piece, piece), piece)

        def place_right(t):
            span = PAIR * piece
            each = PIECES // PAIR
            return t // each, pl.ds(pl.multiple_of(lax.rem(t, each) * span, span), span)

        def right(src, t):
            m, part = place_right(t)
            return pltpu.make_async_remote_copy(
                src.at[m, part], pi.at[m, part], p_s.at[t // (per // PAIR)], p_r.at[t],
                device_id=(hd, tok + 2), device_id_type=MESH,
            )

        def left(src, t):
            m, part = place(t)
            return pltpu.make_async_remote_copy(
                src.at[m, part], si.at[m, part], s_s.at[t // per], s_r.at[t],
                device_id=(hd, tok - 2), device_id_type=MESH,
            )

        def swap(i, k):
            return pltpu.make_async_remote_copy(
                sent.at[i, k], got.at[i, k], sw_s.at[i], sw_r.at[i],
                device_id=partner, device_id_type=MESH,
            )

        def swap_piece(g):
            part = pl.ds(g * piece, piece)
            return pltpu.make_async_remote_copy(
                sent.at[0, 0, part], got.at[0, 0, part], sw_s.at[0], sw_p.at[g],
                device_id=partner, device_id_type=MESH,
            )

        def wide(h):
            return pl.ds(pl.multiple_of((hd * heads + h) * size, size), size)

        def band(peer):
            return pl.ds(pl.multiple_of(peer * share, share), share)

        order = (3, 1, 2, 0) if nh == 4 else tuple(range(nh - 1, -1, -1))

        def other(p):
            if nh != 4 or p == 0:
                return lax.rem(hd + p, nh)
            return (hd + 1 - 2 * lax.rem(hd, 2), lax.rem(hd + 2, 4), 3 - hd)[p - 1]

        def deal(h, p):
            peer = other(p)
            return pltpu.make_async_remote_copy(
                ob.at[h, band(peer)], out.at[0, :, wide(h)], a_s.at[0], a_r.at[p - 1],
                device_id=(peer, tok), device_id_type=MESH,
            )

        def keep(h):
            return pltpu.make_async_copy(ob.at[h, band(hd)], out.at[0, :, wide(h)], a_s.at[1])

        def deal_next(i, c, p):
            peer = other(p)
            return pltpu.make_async_remote_copy(
                ox.at[i, c * nh + peer], out.at[1, :, wide(mine(i))],
                b_s.at[i], b_p.at[i] if p == 0 else b_r.at[p - 1],
                device_id=(peer, 2 * z + c), device_id_type=MESH,
            )

        def keep_next(i):
            return pltpu.make_async_copy(
                ox.at[i, lane * nh + hd], out.at[1, :, wide(mine(i))], b_l.at[i]
            )

        def gradients(h, put, await_early=None, await_late=None):
            if await_early is not None:
                await_early()
            keys = kb[:, cut(h)]
            gate = wf[1, h].astype(BF)
            up = wf[2, h].astype(BF)
            wh[1, h] = gate
            wh[2, h] = up
            zg = mm(keys, gate)
            zu = mm(keys, up)
            sig = 1.0 / (1.0 + jnp.exp(-zg))
            silu = zg * sig
            hidden = (silu * zu).astype(BF)
            if await_late is not None:
                await_late()
            down = wf[0, h].astype(BF)
            wh[0, h] = down
            line = jnp.broadcast_to(rb[pl.ds(h, 1), :], (128, rows))
            column = jnp.transpose(line)
            column = jnp.concatenate([column] * (size // 128), axis=1)
            dout = (-(column * vb[:, cut(h)].astype(F32))).astype(BF)
            put(0, mm_tn(hidden, dout))
            dh = mm_nt(dout, down)
            dzu = (dh * silu).astype(BF)
            dzg = (dh * zu * sig * (1.0 + zg * (1.0 - sig))).astype(BF)
            put(1, mm_tn(keys, dzg))
            put(2, mm_tn(keys, dzu))

        def gradients_theirs(i, before=lambda k: None, waits=()):
            def put(k, part):
                sent[i, k] = part.astype(BF)
                before(k)
                if isinstance(i, int) and k == 0:
                    for g in range(PIECES):
                        swap_piece(g).start()
                else:
                    swap(i, k).start()

            gradients(theirs(i), put, *waits)

        def gradients_mine(i):
            def put(k, part):
                mg[k] = part

            gradients(mine(i), put)

        def add_first():
            for g in range(PIECES):
                part = pl.ds(g * piece, piece)
                swap_piece(g).wait_recv()
                own[0, part] = (mg[0, part] + got[0, 0, part].astype(F32)).astype(BF)

                @pl.when(last_end)
                def _():
                    left(own, g).start()

                if g % PAIR == PAIR - 1:

                    @pl.when(first_end)
                    def _():
                        right(own, g // PAIR).start()

        def add_theirs(i):
            early = isinstance(i, int) and i == 0
            if early:
                add_first()
            begin = 1 if early else 0
            rest_of = got.at[i, pl.ds(begin, KINDS - begin)]
            pltpu.make_async_copy(rest_of, rest_of, sw_r.at[i]).wait()
            for k in range(begin, KINDS):
                own[KINDS * i + k] = (mg[k] + got[i, k].astype(F32)).astype(BF)

                @pl.when(first_end)
                def _():
                    for g in range(PIECES // PAIR):
                        right(own, (KINDS * i + k) * (PIECES // PAIR) + g).start()

                @pl.when(last_end)
                def _():
                    for g in range(PIECES):
                        left(own, per * i + k * PIECES + g).start()

        turn_at = per * (slots - 1)
        alone = (mine(slots - 1) < heads) & (theirs(slots - 1) >= heads)

        def turn(t, far):
            fast = (LAG_ALONE - LAG) * far
            held = jnp.where(t < turn_at + fast, -1, t - LAG_ALONE * far)
            return jnp.where(alone & (t >= turn_at), held, t - LAG * far)

        def pass_on(t):
            @pl.when(middle)
            def _():
                p = turn(t, z - 1)
                s = turn(t, nz - 2 - z)

                @pl.when((p >= 0) & (p < total) & (lax.rem(p, PAIR) == PAIR - 1))
                def _():
                    n = p // PAIR
                    m, part = place_right(n)
                    right(po, n).wait_recv()
                    po[m, part] = (pi[m, part].astype(F32) + own[m, part].astype(F32)).astype(BF)
                    right(po, n).start()

                @pl.when((s >= 0) & (s < total))
                def _():
                    m, part = place(s)
                    left(so, s).wait_recv()
                    so[m, part] = (si[m, part].astype(F32) + own[m, part].astype(F32)).astype(BF)
                    left(so, s).start()

        def first(h):
            ob[h] = fast_apply(qb[:, cut(h)], wh[1, h], wh[2, h], wh[0, h])
            for p in order[:-1]:
                deal(h, p).start()
            keep(h).start()

        def gather_some(i, kinds):
            for k in kinds:
                m = KINDS * i + k

                @pl.when(first_end)
                def _():
                    for g in range(PIECES):
                        part = pl.ds(g * piece, piece)
                        left(own, per * i + k * PIECES + g).wait_recv()
                        xs[k, part] = own[m, part].astype(F32) + si[m, part].astype(F32)

                @pl.when(last_end)
                def _():
                    for g in range(PIECES // PAIR):
                        part = pl.ds(g * PAIR * piece, PAIR * piece)
                        right(own, (KINDS * i + k) * (PIECES // PAIR) + g).wait_recv()
                        xs[k, part] = own[m, part].astype(F32) + pi[m, part].astype(F32)

                @pl.when(middle)
                def _():
                    xs[k] = own[m].astype(F32) + pi[m].astype(F32) + si[m].astype(F32)

            grads = [xs[k] for k in kinds]
            scales = [1.0 / (jnp.sqrt(jnp.sum(v * v)) + 1e-07) for v in grads]
            for k, v, scale in zip(kinds, grads, scales):
                xs[k] = v * scale

        def gather(i):
            gather_some(i, range(KINDS - 1))
            gather_some(i, [KINDS - 1])

        def sweep(i=None):
            x = [xs[k] for k in range(KINDS)]
            xb = [v.astype(BF) for v in x]
            gram = [mm_nt(v, v) for v in xb]
            half = [v.astype(BF) for v in gram]
            square = [mm(v, v) for v in half]
            poly = [(coef_second * a + coef_third * b).astype(BF) for a, b in zip(gram, square)]
            for k in range(KINDS):
                y = coef_first * x[k] + mm(poly[k], xb[k])
                if i is None:
                    xs[k] = y
                else:
                    wn[k] = (wf[k, mine(i)] - y).astype(BF)


        def second(i):
            x = qn[:, :, cut(mine(i))].reshape(2 * rows, size)
            ox[i] = fast_apply(x, wn[1], wn[2], wn[0]).reshape(2 * nh, share, size)
            for p in order:
                for c in range(2):
                    if p > 0:
                        deal_next(i, c, p).start()
                    else:

                        @pl.when(lane != c)
                        def _():
                            deal_next(i, c, p).start()

            keep_next(i).start()

        def ready_theirs(i):
            @pl.when(theirs(i) < heads)
            def _():
                gradients_theirs(i)

        def add_mine(i):
            @pl.when(mine(i) < heads)
            def _():
                add_theirs(i)

        def ready_mine(i):
            @pl.when((i < slots) & (mine(i) < heads))
            def _():
                gradients_mine(i)
                add_theirs(i)

        def first_of(h):
            @pl.when(h < heads)
            def _():
                first(h)

        first_loads = opening()
        for copy in (*first_loads[1:3], first_loads[0], *first_loads[3:]):
            copy.start()

        @pl.when(z > 0)
        def _():
            pl.semaphore_signal(barrier, inc=1, device_id=(hd, tok - 2), device_id_type=MESH)

        @pl.when(z < nz - 1)
        def _():
            pl.semaphore_signal(barrier, inc=1, device_id=(hd, tok + 2), device_id_type=MESH)

        greet_plane()
        load_head(1, cut(mine(0)), pl.ds(mine(0), 1))
        rest = heads - 2

        def early_waits():
            first_loads[0].wait()
            two = wf.at[pl.ds(1, 2), theirs(0)]
            pltpu.make_async_copy(two, two, ld.at[3, 1]).wait()

        def late_waits():
            for copy in first_loads[3:]:
                copy.wait()
            if rest > 0:
                load_head(2, pl.ds(2 * size, rest * size), pl.ds(2, rest))
            load_first.start()
            load_next.start()


        def enter(k):
            if k == 0:
                pl.semaphore_wait(barrier, 1 + 2 * (nh - 1) + inner)

        gradients_theirs(0, enter, (early_waits, late_waits))
        wait_head(1, 1)
        gradients_mine(0)
        add_theirs(0)
        if heads > 2:
            wait_head(2, rest)

            @pl.loop(1, slots)
            def _(i):
                ready_theirs(i)

        push_next.start()
        if slots > 1:

            @pl.when(mine(1) < heads)
            def _():
                gradients_mine(1)

        hops = max(nz - 3, 0)
        late = LAG * hops if turn_at - LAG * hops >= per * (slots - 2) else LAG_ALONE * hops
        behind, offset = late // per, late % per
        defer = middle & (mine(slots - 1) < heads)

        load_both.wait()

        @pl.loop(0, slots + behind)
        def _(r):
            base = per * r
            i = r - 1 - behind

            def done(work):
                def run():
                    @pl.when((i >= 0) & jnp.logical_not(defer & (i == slots - 2)))
                    def _():
                        work()

                return run

            def begin():
                @pl.when(i == 0)
                def _():
                    push_next.wait_recv()

                gather(i)

            start = offset
            stride = max(PIECES // 4, 1)
            work = {stride: [lambda: ready_mine(r + 2)]}
            firsts = (heads + 1) // 2
            for n in range(firsts):
                work[stride * (2 * n + 3)] = [lambda n=n: first_of(firsts * r + n)]
            tail = []
            for n, item in enumerate([begin, None, sweep, sweep, None, lambda: sweep(i), lambda: second(i)]):
                if item is None:
                    continue
                if start + stride * n < per:
                    work.setdefault(start + stride * n, []).append(done(item))
                else:
                    tail.append(done(item))
            for t in range(per):
                pass_on(base + t)
                if t == 0 and slots > 1:

                    @pl.when(r == 0)
                    def _():
                        add_mine(1)

                for item in work.get(t, []):
                    item()
            for item in tail:
                item()

        @pl.when(middle)
        def _():
            @pl.loop(per * (slots + behind), per * slots + LAG_ALONE * hops)
            def _(t):
                pass_on(t)

        @pl.loop(jnp.where(defer, max(slots - 2, 0), slots - 1), slots)
        def _(i):
            @pl.when(mine(i) < heads)
            def _():
                if slots <= 2:

                    @pl.when(i == 0)
                    def _():
                            push_next.wait_recv()

                gather(i)
                for s in range(NS_STEPS):
                    sweep(i if s == NS_STEPS - 1 else None)
                second(i)

        push_next.wait_send()

        @pl.loop(0, slots)
        def _(i):
            @pl.when(theirs(i) < heads)
            def _():
                pltpu.make_async_copy(sent.at[i], sent.at[i], sw_s.at[i]).wait()

            @pl.when(mine(i) < heads)
            def _():
                slot = own.at[pl.ds(KINDS * i, KINDS)]

                @pl.when(z < nz - 1)
                def _():
                    pltpu.make_async_copy(slot, slot, p_s.at[i]).wait()

                @pl.when(z > 0)
                def _():
                    pltpu.make_async_copy(slot, slot, s_s.at[i]).wait()

        @pl.loop(0, slots)
        def _(i):
            part = ox.at[i, 0]

            @pl.when(theirs(i) < heads)
            def _():
                pltpu.make_async_copy(part, part, b_p.at[i]).wait()

            @pl.when(mine(i) < heads)
            def _():
                most = ox.at[i, pl.ds(0, 2 * nh - 1)]
                pltpu.make_async_copy(most, most, b_s.at[i]).wait()
                pltpu.make_async_copy(part, part, b_l.at[i]).wait()

        part = ob.at[:, pl.ds(0, (nh - 1) * share)]
        pltpu.make_async_copy(part, part, a_s.at[0]).wait()
        part = ob.at[:, pl.ds(0, share)]
        pltpu.make_async_copy(part, part, a_s.at[1]).wait()
        for p in range(1, nh):
            part = out.at[0, :, pl.ds(0, heads * size)]
            pltpu.make_async_copy(part, part, a_r.at[p - 1]).wait()
            part = out.at[1, :, pl.ds(0, heads * size)]
            pltpu.make_async_copy(part, part, b_r.at[p - 1]).wait()

    dma = pltpu.SemaphoreType.DMA
    pieces = KINDS * slots * PIECES
    pl.run_scoped(
        main,
        dma((5, 2)), dma((2,)),
        dma((slots,)), dma((PIECES,)), dma((slots,)),
        dma((slots,)), dma((pieces // PAIR,)),
        dma((slots,)), dma((pieces,)),
        dma((2,)), dma((nh - 1,)),
        dma((slots,)), dma((nh - 1,)), dma((slots,)), dma((slots,)),
    )


def solution(mesh):
    nh = mesh.shape["head"]
    nz = mesh.shape["tok"] // 2

    def local(queries, key_rows, value_rows, step_rates, gate_fast, up_fast, down_fast):
        heads, size, _ = gate_fast.shape
        rows = key_rows.shape[0]
        slots = (heads + 1) // 2
        matrices = KINDS * slots
        out_shape = (2, rows // nh, nh * heads * size)
        out_bytes = 2 * out_shape[0] * out_shape[1] * out_shape[2]
        anywhere = pl.BlockSpec(memory_space=pl.ANY)
        stack = pltpu.VMEM((matrices, size, size), BF)
        return pl.pallas_call(
            functools.partial(kernel, nh, nz),
            out_shape=pltpu.VMEM(out_shape, BF),
            in_specs=[anywhere] * 7,
            out_specs=pl.BlockSpec(memory_space=pltpu.VMEM),
            scratch_shapes=[
                pltpu.VMEM((rows, heads * size), BF),
                pltpu.VMEM((2, rows, heads * size), BF),
                pltpu.VMEM((rows, heads * size), BF),
                pltpu.VMEM((rows, heads * size), BF),
                pltpu.VMEM((heads, rows), F32),
                pltpu.VMEM((KINDS, heads, size, size), F32),
                pltpu.VMEM((KINDS, heads, size, size), BF),
                stack,
                pltpu.VMEM((slots, KINDS, size, size), BF),
                pltpu.VMEM((slots, KINDS, size, size), BF),
                stack, stack, stack, stack,
                pltpu.VMEM((KINDS, size, size), F32),
                pltpu.VMEM((KINDS, size, size), F32),
                pltpu.VMEM((KINDS, size, size), BF),
                pltpu.VMEM((heads, rows, size), BF),
                pltpu.VMEM((slots, 2 * nh, rows // nh, size), BF),
            ],
            compiler_params=pltpu.CompilerParams(
                collective_id=0,
                has_side_effects=True,
                vmem_limit_bytes=VMEM_BYTES - out_bytes - 16384,
            ),
        )(queries, key_rows, value_rows, step_rates, gate_fast, up_fast, down_fast)

    placed = (
        P(None, "tok", "head"),
        P("tok", "head"),
        P("tok", "head"),
        P("head", "tok"),
        P("head", None, None),
        P("head", None, None),
        P("head", None, None),
    )
    return jax.shard_map(
        local, mesh=mesh, in_specs=placed, out_specs=P(None, ("tok", "head"), None), check_vma=False
    )
```
